128 devices in a mesh: ep: 32 (over z, y, core), sp: 4 (over x).
Axes of the slice: x: 4, y: 4, z: 4, core: 2. Of those that a mesh axis runs over, the one named last changes fastest.
Arguments:
- hidden_in: bfloat16 [16384, 6656], P(('ep', 'sp')), may hold values from -6 to 6
- grad_out: bfloat16 [16384, 6656], P(('ep', 'sp')), may hold values from -6 to 6
- route_ids: int32 [16384, 8], P(('ep', 'sp')), may hold values from 0 to 255, all different within a row; in each aligned block of 128 rows (0 to 127, 128 to 255, ...) at most 6 rows name the same one
- route_probs: float32 [16384, 8], P(('ep', 'sp')), may hold values from 0.05 to 0.6
- w_gate: bfloat16 [32, 6656, 1024], P('ep', 'sp'), may hold values from -0.078125 to 0.078125
- w_up: bfloat16 [32, 6656, 1024], P('ep', 'sp'), may hold values from -0.078125 to 0.078125
- w_down: bfloat16 [32, 1024, 6656], P('ep', None, 'sp'), may hold values from -0.1875 to 0.1875
Outputs:
- grad_in: bfloat16 [16384, 6656], P(('ep', 'sp'))
- grad_w_gate: bfloat16 [32, 6656, 1024], P('ep', 'sp')
- grad_w_up: bfloat16 [32, 6656, 1024], P('ep', 'sp')
- grad_w_down: bfloat16 [32, 1024, 6656], P('ep', None, 'sp')
- grad_probs: bfloat16 [16384, 8], P(('ep', 'sp'))
The draws below stay inside these ranges and needn't reach their ends.
Inputs may be any that keep to these rules, and one draw needn't show every extreme that they name: `route_ids`: each row names 8 different routed experts; only those below 32 belong to the window. In each aligned block of 128 rows (the rows of one device) no routed expert is named by more than 6 rows, a bound that some block reaches.
All inputs are finite; a program needn't handle non-finite values.
Results may differ from the reference program's by a relative error of at most 0.03.
Values may be sent and summed in bfloat16 or wider, within the bound.
No kernel may reach another device: no remote copies, remote signals or barrier semaphores. Data moves between devices by JAX's collectives and lax.ppermute only.
A program may use at most 128 MiB of HBM per device.

```python
import math
import jax
import jax.numpy as jnp
import numpy as np
from jax import lax

D = 6656
FF = 1024
ROUTED = 256
TOP = 8
TOK_DEV = 128
EXPERTS = 32
CAP = 6
TOKENS = 16384
N_SP = 4


def level_of(stream_key, extent, shards, least, largest):
    level, own = 1.0, jax.random.fold_in(stream_key, 6)
    for dim, blocks in shards:
        heights = jnp.exp(jax.random.uniform(jax.random.fold_in(own, dim), (blocks,), jnp.float32, least / len(shards), largest / len(shards)))
        level = level * jnp.repeat(heights, extent[dim] // blocks).reshape([-1 if axis == dim else 1 for axis in range(len(extent))])
    return level


def deal_out(stream_key, own, number, rows, amount, top, limit, lean):
    sequence = jax.random.permutation(stream_key, amount)
    crowded, usual = shares(amount, rows * top, limit, lean, True), shares(amount, rows * top, limit, lean, False)
    places = jnp.arange(amount)

    def named(sizes, turn):
        used = int((sizes > 0).sum())
        fixed = max(1, used // 4)
        passed = fixed + (places - fixed + turn * (used - fixed)) % max(1, amount - fixed)
        return jnp.zeros((amount,), jnp.int32).at[sequence[jnp.where(places < fixed, places, passed)]].set(jnp.asarray(sizes, jnp.int32))

    sizes = jnp.where(number % 4 == 0, named(crowded, number // 4), named(usual, number - number // 4 - 1))
    mixed = jax.random.permutation(jax.random.fold_in(own, 3), amount)
    source_of, taker = mixed[0:amount // 2 * 2:2], mixed[1:amount // 2 * 2:2]
    slack = jnp.minimum(sizes[source_of] - 1, limit - sizes[taker]) // 2
    slack = jnp.where((source_of == sequence[0]) | (taker == sequence[0]) | (sizes[taker] == 0), 0, jnp.maximum(slack, 0))
    passed = jax.random.randint(jax.random.fold_in(own, 4), (amount // 2,), 0, 1 << 20) % (slack + 1)
    sizes = sizes.at[source_of].add(-passed).at[taker].add(passed)
    members = jnp.searchsorted(jnp.cumsum(sizes), jnp.arange(rows * top), side="right").astype(jnp.int32)
    listing = members.reshape(top, rows).T
    listing = listing[jax.random.permutation(jax.random.fold_in(own, 1), rows)]
    turn = jax.random.randint(jax.random.fold_in(own, 2), (rows, 1), 0, top)
    return jnp.take_along_axis(listing, (jnp.arange(top)[None, :] + turn) % top, axis=1)


def shares(amount, total, bound, skew, full):
    weights = [(1 << 20) // math.isqrt(standing ** skew) + 1 for standing in range(1, amount + 1)]
    largest = bound if full else min(bound, max(-(-total // amount), total * weights[0] // sum(weights)))
    least = 1 if total - largest >= amount - 1 else 0
    given, surplus = [largest] + [least] * (amount - 1), total - largest - least * (amount - 1)
    while surplus > 0:
        free = [i for i in range(1, amount) if given[i] < largest] or [i for i in range(1, amount) if given[i] < bound]
        pool, remaining = sum([weights[i] for i in free]), surplus
        for i in free:
            more = min(bound - given[i], max(1, remaining * weights[i] // pool), surplus)
            given[i] = given[i] + more
            surplus = surplus - more
    return np.array(given)


def scatter_about(stream_key, shape, deviation, limit, shards=(), kind=jnp.bfloat16):
    result = jax.random.normal(stream_key, shape, jnp.float32) * deviation
    if len(shards) > 0:
        result = level_of(stream_key, shape, shards, -0.22, 0.18) * result
    return jnp.clip(result, min=-limit, max=limit).astype(kind)


def setup_inputs(seed: int = 0) -> dict:
    arg_keys = jax.random.split(jax.random.key(seed), 8)
    hidden_in = scatter_about(arg_keys[0], (TOKENS, D), 1.0, 6.0, ((0, 128),))
    grad_out = scatter_about(arg_keys[1], (TOKENS, D), 1.0, 6.0, ((0, 128),))
    route_ids_keys = jax.random.split(jax.random.fold_in(arg_keys[2], 1), TOKENS // TOK_DEV)
    route_ids_turns = jax.random.permutation(jax.random.fold_in(arg_keys[2], 3), TOKENS // TOK_DEV)
    route_ids = jax.vmap(lambda own, number: deal_out(jax.random.fold_in(arg_keys[2], 2), own, number, TOK_DEV, ROUTED, TOP, CAP, 2))(route_ids_keys, route_ids_turns).reshape((TOKENS, TOP))
    route_probs = jnp.clip(0.05 + 0.55 * jax.random.uniform(arg_keys[3], (TOKENS, TOP), jnp.float32) ** level_of(arg_keys[3], (TOKENS, TOP), ((0, 128),), -0.2, 0.2), 0.05, 0.6)
    w_gate = scatter_about(arg_keys[4], (EXPERTS, D, FF), D ** -0.5, 0.078125, ((0, 32), (1, 4)))
    w_up = scatter_about(arg_keys[5], (EXPERTS, D, FF), D ** -0.5, 0.078125, ((0, 32), (1, 4)))
    w_down = scatter_about(arg_keys[6], (EXPERTS, FF, D), FF ** -0.5, 0.1875, ((0, 32), (2, 4)))
    return dict(hidden_in=hidden_in, grad_out=grad_out, route_ids=route_ids, route_probs=route_probs, w_gate=w_gate, w_up=w_up, w_down=w_down)


def slot_tables(route_ids, route_probs):
    blocks = route_ids.shape[0] // TOK_DEV
    flat_ids = route_ids.reshape(blocks, TOK_DEV * TOP)
    inside = flat_ids < EXPERTS
    onehot = (flat_ids[:, :, None] == jnp.arange(EXPERTS, dtype=jnp.int32)[None, None, :]).astype(jnp.int32)
    slot_rank = jnp.sum((jnp.cumsum(onehot, axis=1) - onehot) * onehot, axis=2)
    per_expert = blocks * CAP
    block_ids = jnp.arange(blocks, dtype=jnp.int32)[:, None]
    slot_index = jnp.where(inside, flat_ids * per_expert + block_ids * CAP + slot_rank, EXPERTS * per_expert)
    slot_index = slot_index.reshape(-1).astype(jnp.int32)
    token_ids = (jnp.arange(blocks * TOK_DEV * TOP, dtype=jnp.int32) // TOP).astype(jnp.int32)
    source_rows = jnp.full((EXPERTS * per_expert + 1,), blocks * TOK_DEV, jnp.int32).at[slot_index].set(token_ids)[:-1]
    slot_weights = jnp.zeros((EXPERTS * per_expert + 1,), jnp.float32).at[slot_index].set(route_probs.reshape(-1))[:-1]
    return slot_index, source_rows.reshape(EXPERTS, per_expert), slot_weights.reshape(EXPERTS, per_expert)


def quarter_sum(parts):
    rounded = lax.optimization_barrier(parts.astype(jnp.bfloat16))
    return jnp.sum(rounded.astype(jnp.float32), axis=0)


def expert_grads(x_rows, dy_rows, slot_weights, gate_weight, up_weight, down_weight):
    row_count = x_rows.shape[0]
    quarter = gate_weight.shape[0] // N_SP
    x_four = x_rows.reshape(row_count, N_SP, quarter).astype(jnp.float32)
    dy_four = dy_rows.reshape(row_count, N_SP, quarter).astype(jnp.float32)
    gate_parts = jnp.einsum('rqd,qdf->qrf', x_four, gate_weight.reshape(N_SP, quarter, FF).astype(jnp.float32))
    up_parts = jnp.einsum('rqd,qdf->qrf', x_four, up_weight.reshape(N_SP, quarter, FF).astype(jnp.float32))
    back_parts = jnp.einsum('rqd,fqd->qrf', dy_four, down_weight.reshape(FF, N_SP, quarter).astype(jnp.float32))
    gate_sum = quarter_sum(gate_parts)
    up_sum = quarter_sum(up_parts)
    back_sum = quarter_sum(back_parts)
    weight = lax.optimization_barrier(slot_weights.astype(jnp.bfloat16)).astype(jnp.float32)[:, None]
    sigmoid_gate = jax.nn.sigmoid(gate_sum)
    activation = gate_sum * sigmoid_gate * up_sum
    grad_act = weight * back_sum
    grad_gate = (grad_act * up_sum * sigmoid_gate * (1.0 + gate_sum * (1.0 - sigmoid_gate))).astype(jnp.bfloat16)
    grad_up = (grad_act * gate_sum * sigmoid_gate).astype(jnp.bfloat16)
    weighted = (weight * activation).astype(jnp.bfloat16)
    slot_prob = jnp.sum(back_sum * activation, axis=1).astype(jnp.bfloat16)
    grad_gate_weight = jnp.dot(x_rows.T, grad_gate, preferred_element_type=jnp.float32).astype(jnp.bfloat16)
    grad_up_weight = jnp.dot(x_rows.T, grad_up, preferred_element_type=jnp.float32).astype(jnp.bfloat16)
    grad_down_weight = jnp.dot(weighted.T, dy_rows, preferred_element_type=jnp.float32).astype(jnp.bfloat16)
    row_grad = jnp.dot(grad_gate, gate_weight.T, preferred_element_type=jnp.float32)
    row_grad = (row_grad + jnp.dot(grad_up, up_weight.T, preferred_element_type=jnp.float32)).astype(jnp.bfloat16)
    return grad_gate_weight, grad_up_weight, grad_down_weight, row_grad, slot_prob


def reference(hidden_in, grad_out, route_ids, route_probs, w_gate, w_up, w_down):
    token_count = hidden_in.shape[0]
    slot_index, source_rows, slot_weights = slot_tables(route_ids, route_probs)
    x_ext = jnp.concatenate([hidden_in, jnp.zeros((1, D), jnp.bfloat16)], axis=0)
    dy_ext = jnp.concatenate([grad_out, jnp.zeros((1, D), jnp.bfloat16)], axis=0)

    def expert_step(accum, inputs):
        sources, weights, gate_weight, up_weight, down_weight = inputs
        outputs = expert_grads(x_ext[sources], dy_ext[sources], weights, gate_weight, up_weight, down_weight)
        accum = accum.at[sources].add(outputs[3].astype(jnp.float32))
        return accum, (outputs[0], outputs[1], outputs[2], outputs[4])

    start_accum = jnp.zeros((token_count + 1, D), jnp.float32)
    accum, stacked = lax.scan(expert_step, start_accum, (source_rows, slot_weights, w_gate, w_up, w_down))
    grad_in = accum[:-1].astype(jnp.bfloat16)
    prob_flat = jnp.concatenate([stacked[3].reshape(-1), jnp.zeros((1,), jnp.bfloat16)], axis=0)
    grad_probs = prob_flat[slot_index].reshape(token_count, TOP)
    return grad_in, stacked[0], stacked[1], stacked[2], grad_probs
```

```python
import functools

import jax
import jax.numpy as jnp
from jax import lax
from jax.experimental import pallas as pl
from jax.experimental.pallas import tpu as pltpu
from jax.sharding import PartitionSpec as P

CAP = 6
EXPERTS = 32
TOK = 128
TOP = 8
WIDE = 1280
TAIL = 384
QUARTER = WIDE + TAIL
PACKED = 8
BLOCK = 32
SLOTS = BLOCK * CAP
ROWS8 = BLOCK * PACKED
MIB = 1 << 20
BF16 = jnp.bfloat16
F32 = jnp.float32


def iota(shape, dim):
    return lax.broadcasted_iota(jnp.int32, shape, dim)


def product(a, b):
    return jnp.dot(a, b, preferred_element_type=F32)


def product_t(a, b):
    return lax.dot_general(a, b, (((1,), (1,)), ((), ())), preferred_element_type=F32)


def one_hot(mask):
    return jnp.where(mask, 1.0, 0.0)


def tables(ids, probs, left_ref, combine_ref, spare_ref):
    lane = iota((TOK, 128), 1)
    member = jnp.zeros((TOK, 128), F32)
    weight = jnp.zeros((TOK, 128), F32)
    for k in range(TOP):
        hit = ids[:, k : k + 1] == lane
        member = member + jnp.where(hit, 1.0, 0.0)
        weight = weight + jnp.where(hit, probs[:, k : k + 1], 0.0)
    member = member.astype(BF16)
    before = one_hot(iota((TOK, TOK), 1) < iota((TOK, TOK), 0)).astype(BF16)
    rank = product(before, member).astype(BF16)
    widen = one_hot(iota((128, ROWS8), 0) == iota((128, ROWS8), 1) // PACKED).astype(BF16)
    member8 = product(member, widen)
    rank8 = product(rank, widen)
    weight8 = product(weight.astype(BF16), widen)
    place = iota((TOK, ROWS8), 1) % PACKED
    rank8 = jnp.where(member8 > 0.5, rank8, -1.0)
    own = one_hot((rank8 == place.astype(F32)) & (place < CAP))
    combine_ref[0] = own.astype(BF16)
    own_t = own.T
    for g in range(3):
        goal = (place - CAP) * 3 + g
        tail = one_hot((rank8 == goal.astype(F32)) & (place >= CAP))
        combine_ref[g + 1] = tail.astype(BF16)
        left_ref[g] = jnp.concatenate([own_t, tail.T], axis=1).astype(BF16)
    prob = jnp.sum(own_t * weight8.T, axis=1, keepdims=True)
    row = iota((ROWS8, 128), 0)
    diagonal = jnp.where(row % PACKED == iota((ROWS8, 128), 1), prob, 0.0).astype(BF16)
    r = iota((ROWS8, ROWS8), 0)
    c = iota((ROWS8, ROWS8), 1)
    lift = one_hot((r // PACKED == c // PACKED) & (r % PACKED == CAP)).astype(BF16)
    spare_ref[...] = product(lift, diagonal).astype(BF16)


def spread(left_ref, x_ref, out_ref):
    rest = x_ref[:, WIDE:]
    for g in range(3):
        cols = pl.ds(g * TAIL, TAIL)
        right = jnp.concatenate([x_ref[:, cols], rest], axis=0)
        out_ref[:, cols] = product(left_ref[g], right).astype(BF16)
    return product(left_ref[0][:, :TOK], x_ref[:, 3 * TAIL : WIDE])


def spread_x_kernel(ids_ref, probs_ref, x_ref, out_ref, left_ref, combine_ref, spare_ref):
    @pl.when(pl.program_id(0) == 0)
    def _():
        tables(ids_ref[...], probs_ref[...], left_ref, combine_ref, spare_ref)

    out_ref[:, 3 * TAIL :] = spread(left_ref, x_ref, out_ref).astype(BF16)


def spread_dy_kernel(left_ref, spare_ref, x_ref, out_ref):
    last = spread(left_ref, x_ref, out_ref)
    out_ref[:, 3 * TAIL :] = last.astype(BF16) + spare_ref[...]


def unpack_masks(main_ref, tail_ref):
    r = iota((SLOTS, ROWS8), 0)
    c = iota((SLOTS, ROWS8), 1)
    same = r // CAP == c // PACKED
    slot = r % CAP
    place = c % PACKED
    main_ref[...] = one_hot(same & (slot == place)).astype(BF16)
    for g in range(3):
        tail = one_hot(same & (place >= CAP) & (slot == (place - CAP) * 3 + g))
        tail_ref[:, g * ROWS8 : (g + 1) * ROWS8] = tail.astype(BF16)


def stacked(packed):
    return jnp.concatenate([packed[:, g * TAIL : (g + 1) * TAIL] for g in range(3)], axis=0)


def unpack(main_ref, tail_ref, packed, rows_ref):
    rows_ref[:, :WIDE] = product(main_ref[...], packed).astype(BF16)
    rows_ref[:, WIDE:] = product(tail_ref[...], stacked(packed)).astype(BF16)


def gate_up_kernel(packed_ref, gate_ref, up_ref, rows_ref, parts_ref, main_ref, tail_ref):
    @pl.when(pl.program_id(0) == 0)
    def _():
        unpack_masks(main_ref, tail_ref)

    unpack(main_ref, tail_ref, packed_ref[...], rows_ref)
    rows = rows_ref[...]
    hidden = gate_ref.shape[1]
    parts_ref[:, :hidden] = product(rows, gate_ref[...]).astype(BF16)
    parts_ref[:, hidden:] = product(rows, up_ref[...]).astype(BF16)


def back_kernel(packed_ref, down_ref, rows_ref, part_ref, prob_ref, main_ref, tail_ref):
    @pl.when(pl.program_id(0) == 0)
    def _():
        unpack_masks(main_ref, tail_ref)

    packed = packed_ref[...]
    unpack(main_ref, tail_ref, packed, rows_ref)
    part_ref[...] = product_t(rows_ref[...], down_ref[...]).astype(BF16)
    r = iota((SLOTS, ROWS8), 0)
    c = iota((SLOTS, ROWS8), 1)
    pick = one_hot((r // CAP == c // PACKED) & (c % PACKED == CAP)).astype(BF16)
    probs = product(pick, packed[:, 3 * TAIL :])
    mine = iota((SLOTS, 128), 0) % CAP == iota((SLOTS, 128), 1)
    prob = jnp.sum(jnp.where(mine, probs, 0.0), axis=1, keepdims=True)
    prob_ref[...] = jnp.broadcast_to(prob, (SLOTS, 128)).astype(BF16)


def activate_kernel(gate_up_ref, back_ref, prob_ref, grads_ref, weighted_ref, slot_ref):
    hidden = back_ref.shape[1]
    gate = gate_up_ref[:, :hidden].astype(F32)
    up = gate_up_ref[:, hidden:].astype(F32)
    back = back_ref[...].astype(F32)
    weight = prob_ref[:, :1].astype(F32)
    sigmoid = 1.0 / (1.0 + jnp.exp(-gate))
    swish = gate * sigmoid
    act = swish * up
    grad_act = weight * back
    grads_ref[:, :hidden] = (grad_act * up * sigmoid * (1.0 + gate * (1.0 - sigmoid))).astype(BF16)
    grads_ref[:, hidden:] = (grad_act * swish).astype(BF16)
    weighted_ref[...] = (weight * act).astype(BF16)
    slot = jnp.sum(back * act, axis=1, keepdims=True)
    shape = slot_ref.shape
    mine = iota(shape, 0) % CAP == iota(shape, 1)
    slot_ref[...] = jnp.where(mine, slot, 0.0).astype(BF16)


def row_grad_kernel(own_ref, grads_ref, gate_ref, up_ref, slot_ref, out_ref, pack_ref, lift_ref):
    @pl.when(pl.program_id(0) == 0)
    def _():
        r = iota((ROWS8, SLOTS), 0)
        c = iota((ROWS8, SLOTS), 1)
        same = r // PACKED == c // CAP
        place = r % PACKED
        slot = c % CAP
        for g in range(3):
            pack_ref[g, :, :SLOTS] = one_hot(same & (slot == place)).astype(BF16)
            tail = one_hot(same & (place >= CAP) & (slot == (place - CAP) * 3 + g))
            pack_ref[g, :, SLOTS:] = tail.astype(BF16)
        lift_ref[...] = one_hot(same & (place == CAP)).astype(BF16)

    hidden = gate_ref.shape[1]
    rows = product_t(grads_ref[:, :hidden], gate_ref[...])
    rows = (rows + product_t(grads_ref[:, hidden:], up_ref[...])).astype(BF16)
    rest = rows[:, WIDE:]
    for g in range(3):
        right = jnp.concatenate([rows[:, g * TAIL : (g + 1) * TAIL], rest], axis=0)
        out_ref[:, g * TAIL : (g + 1) * TAIL] = product(pack_ref[g], right).astype(BF16)
    last = product(pack_ref[0, :, :SLOTS], rows[:, 3 * TAIL : WIDE])
    held = jnp.where(own_ref[0] == pl.program_id(0), 1.0, 0.0)
    last = last + held * product(lift_ref[...], slot_ref[...])
    out_ref[:, 3 * TAIL :] = last.astype(BF16)


def combine_kernel(ids_ref, combine_ref, packed_ref, out_ref, probs_ref, slot_ref):
    step = pl.program_id(0)
    packed = packed_ref[...]
    out_ref[:, :WIDE] = product(combine_ref[0], packed).astype(BF16)
    tails = jnp.concatenate([combine_ref[g + 1] for g in range(3)], axis=1)
    out_ref[:, WIDE:] = product(tails, stacked(packed)).astype(BF16)
    spare = packed[:, 3 * TAIL :].astype(F32)

    @pl.when(step == 0)
    def _():
        slot_ref[...] = spare

    @pl.when(step > 0)
    def _():
        slot_ref[...] += spare

    @pl.when(step == pl.num_programs(0) - 1)
    def _():
        row = iota((ROWS8, 128), 0)
        slots = jnp.where(row % PACKED == CAP, slot_ref[...], 0.0).astype(BF16)
        r = iota((ROWS8, ROWS8), 0)
        c = iota((ROWS8, ROWS8), 1)
        group = one_hot(r // PACKED == c // PACKED).astype(BF16)
        wide = lax.dot_general(slots, group, (((0,), (0,)), ((), ())), preferred_element_type=F32)
        mine = iota((128, ROWS8), 0) == iota((128, ROWS8), 1) % PACKED
        flat = jnp.sum(jnp.where(mine, wide, 0.0), axis=0, keepdims=True)
        value = (combine_ref[0].astype(F32) * flat).astype(BF16)
        gather = one_hot(iota((ROWS8, 128), 0) // PACKED == iota((ROWS8, 128), 1)).astype(BF16)
        table = product(value, gather)
        lane = iota((TOK, 128), 1)
        for k in range(TOP):
            hit = (ids_ref[:, k : k + 1] == lane) & (lane < EXPERTS)
            found = jnp.sum(jnp.where(hit, table, 0.0), axis=1, keepdims=True)
            probs_ref[:, k : k + 1] = found.astype(BF16)


def call(kernel, grid, ins, outs, scratch=(), flops=0, moved=0):
    return pl.pallas_call(
        kernel,
        grid=(grid,),
        in_specs=ins,
        out_specs=[s for s, _ in outs],
        out_shape=[jax.ShapeDtypeStruct(shape, kind) for _, (shape, kind) in outs],
        scratch_shapes=list(scratch),
        compiler_params=pltpu.CompilerParams(
            dimension_semantics=("arbitrary",), vmem_limit_bytes=48 * MIB
        ),
        cost_estimate=pl.CostEstimate(flops=flops, bytes_accessed=moved, transcendentals=0),
    )


def whole(*shape):
    return pl.BlockSpec(shape, lambda i: (0,) * len(shape))


def once(*shape):
    return pl.BlockSpec(shape, lambda i: (0,) * len(shape), pipeline_mode=pl.Buffered(1))


def rows_of(rows, cols):
    return pl.BlockSpec((rows, cols), lambda i: (i, 0))


def cols_of(rows, cols):
    return pl.BlockSpec((rows, cols), lambda i: (0, i))


def on_device(hidden_in, grad_out, route_ids, route_probs, w_gate, w_up, w_down):
    sp_count = lax.axis_size("sp")
    pieces = lax.axis_size("ep") * sp_count
    hidden = w_gate.shape[2]
    model = hidden_in.shape[1]
    all_rows = pieces * CAP
    packed8 = pieces * PACKED
    gate_weight, up_weight, down_weight = w_gate[0], w_up[0], w_down[0]
    packet = (rows_of(ROWS8, WIDE), ((packed8, WIDE), BF16))
    x_send, left, combine, spare = call(
        spread_x_kernel,
        sp_count,
        [whole(TOK, TOP), whole(TOK, TOP), cols_of(TOK, QUARTER)],
        [
            packet,
            (whole(3, ROWS8, ROWS8), ((3, ROWS8, ROWS8), BF16)),
            (whole(4, TOK, ROWS8), ((4, TOK, ROWS8), BF16)),
            (whole(ROWS8, 128), ((ROWS8, 128), BF16)),
        ],
        flops=2 * packed8 * WIDE * 256,
        moved=2 * (packed8 * WIDE + TOK * model),
    )(route_ids, route_probs, hidden_in)
    (dy_send,) = call(
        spread_dy_kernel,
        sp_count,
        [whole(3, ROWS8, ROWS8), whole(ROWS8, 128), cols_of(TOK, QUARTER)],
        [packet],
        flops=2 * packed8 * WIDE * 256,
        moved=2 * (packed8 * WIDE + TOK * model),
    )(left, spare, grad_out)

    def exchange(packed):
        pieced = packed.reshape(pieces, PACKED, WIDE)
        moved = lax.all_to_all(pieced, ("sp", "ep"), split_axis=0, concat_axis=0, tiled=True)
        return moved.reshape(packed8, WIDE)

    x_packed = exchange(x_send)
    dy_packed = exchange(dy_send)
    masks = (pltpu.VMEM((SLOTS, ROWS8), BF16), pltpu.VMEM((SLOTS, 3 * ROWS8), BF16))
    rows_out = (rows_of(SLOTS, QUARTER), ((all_rows, QUARTER), BF16))
    x_rows, gate_up_part = call(
        gate_up_kernel,
        sp_count,
        [rows_of(ROWS8, WIDE), once(QUARTER, hidden), once(QUARTER, hidden)],
        [rows_out, (rows_of(SLOTS, 2 * hidden), ((all_rows, 2 * hidden), BF16))],
        masks,
        flops=4 * all_rows * QUARTER * hidden,
        moved=2 * (packed8 * WIDE + 2 * QUARTER * hidden + all_rows * (QUARTER + 2 * hidden)),
    )(x_packed, gate_weight, up_weight)
    gate_up = lax.psum_scatter(gate_up_part, "sp", scatter_dimension=0, tiled=True)
    dy_rows, back_part, prob_rows = call(
        back_kernel,
        sp_count,
        [rows_of(ROWS8, WIDE), once(hidden, QUARTER)],
        [
            rows_out,
            (rows_of(SLOTS, hidden), ((all_rows, hidden), BF16)),
            (rows_of(SLOTS, 128), ((all_rows, 128), BF16)),
        ],
        masks,
        flops=2 * all_rows * QUARTER * hidden,
        moved=2 * (packed8 * WIDE + QUARTER * hidden + all_rows * (QUARTER + hidden)),
    )(dy_packed, down_weight)
    back = lax.psum_scatter(back_part, "sp", scatter_dimension=0, tiled=True)
    own = lax.axis_index("sp").astype(jnp.int32)
    own_rows = all_rows // sp_count
    prob_own = lax.dynamic_slice_in_dim(prob_rows, own * own_rows, own_rows, axis=0)
    parts = 4
    step_rows = own_rows // parts
    grads_own, weighted_own, slot_own = call(
        activate_kernel,
        parts,
        [rows_of(step_rows, 2 * hidden), rows_of(step_rows, hidden), rows_of(step_rows, 128)],
        [
            (rows_of(step_rows, 2 * hidden), ((own_rows, 2 * hidden), BF16)),
            (rows_of(step_rows, hidden), ((own_rows, hidden), BF16)),
            (rows_of(step_rows, 128), ((own_rows, 128), BF16)),
        ],
        flops=20 * own_rows * hidden,
        moved=12 * own_rows * hidden,
    )(gate_up, back, prob_own)
    grads = lax.all_gather(grads_own, "sp", axis=0, tiled=True)
    weighted = lax.all_gather(weighted_own, "sp", axis=0, tiled=True)
    (back_send,) = call(
        row_grad_kernel,
        sp_count,
        [
            pl.BlockSpec(memory_space=pltpu.SMEM),
            rows_of(SLOTS, 2 * hidden),
            once(QUARTER, hidden),
            once(QUARTER, hidden),
            whole(SLOTS, 128),
        ],
        [packet],
        (pltpu.VMEM((3, ROWS8, 2 * SLOTS), BF16), pltpu.VMEM((ROWS8, SLOTS), BF16)),
        flops=4 * all_rows * QUARTER * hidden,
        moved=2 * (packed8 * WIDE + 2 * QUARTER * hidden + all_rows * 2 * hidden),
    )(own.reshape(1), grads, gate_weight, up_weight, slot_own)
    back_packed = exchange(back_send)
    contract_rows = (((0,), (0,)), ((), ()))

    def over_rows(a, b):
        return lax.dot_general(a, b, contract_rows, preferred_element_type=F32).astype(BF16)

    grad_gate_weight = over_rows(x_rows, grads[:, :hidden])
    grad_up_weight = over_rows(x_rows, grads[:, hidden:])
    grad_down_weight = over_rows(weighted, dy_rows)
    grad_in, grad_probs = call(
        combine_kernel,
        sp_count,
        [whole(TOK, TOP), whole(4, TOK, ROWS8), rows_of(ROWS8, WIDE)],
        [
            (cols_of(TOK, QUARTER), ((TOK, model), BF16)),
            (whole(TOK, TOP), ((TOK, TOP), BF16)),
        ],
        (pltpu.VMEM((ROWS8, 128), F32),),
        flops=2 * packed8 * WIDE * TOK * 2,
        moved=2 * (packed8 * WIDE + TOK * model),
    )(route_ids, combine, back_packed)
    return (
        grad_in,
        grad_gate_weight[None],
        grad_up_weight[None],
        grad_down_weight[None],
        grad_probs,
    )


def solution(mesh):
    placed = (
        P(("ep", "sp"), None),
        P(("ep", "sp"), None),
        P(("ep", "sp"), None),
        P(("ep", "sp"), None),
        P("ep", "sp", None),
        P("ep", "sp", None),
        P("ep", None, "sp"),
    )
    return jax.shard_map(
        on_device,
        mesh=mesh,
        in_specs=placed,
        out_specs=(
            P(("ep", "sp"), None),
            P("ep", "sp", None),
            P("ep", "sp", None),
            P("ep", None, "sp"),
            P(("ep", "sp"), None),
        ),
        check_vma=False,
    )
```

```python
import jax
import jax.numpy as jnp
from jax import lax
from jax.experimental import pallas as pl
from jax.experimental.pallas import tpu as pltpu
from jax.sharding import PartitionSpec as P

CAP = 6
EXPERTS = 32
TOK = 128
TOP = 8
WIDE = 1280
TAIL = 384
QUARTER = WIDE + TAIL
PACKED = 8
BLOCK = 32
SLOTS = BLOCK * CAP
ROWS8 = BLOCK * PACKED
MIB = 1 << 20
BF16 = jnp.bfloat16
F32 = jnp.float32


def iota(shape, dim):
    return lax.broadcasted_iota(jnp.int32, shape, dim)


def product(a, b):
    return jnp.dot(a, b, preferred_element_type=F32)


def product_t(a, b):
    return lax.dot_general(a, b, (((1,), (1,)), ((), ())), preferred_element_type=F32)


def one_hot(mask):
    return jnp.where(mask, 1.0, 0.0)


def tables(ids, probs, left_ref, combine_ref, spare_ref):
    expert = iota((EXPERTS, TOK), 0)
    member = jnp.zeros((EXPERTS, TOK), F32)
    weight = jnp.zeros((EXPERTS, TOK), F32)
    for k in range(TOP):
        hit = ids[k : k + 1, :] == expert
        member = member + jnp.where(hit, 1.0, 0.0)
        weight = weight + jnp.where(hit, probs[k : k + 1, :], 0.0)
    member = member.astype(BF16)
    before = one_hot(iota((TOK, TOK), 0) < iota((TOK, TOK), 1)).astype(BF16)
    rank = product(member, before).astype(BF16)
    widen = one_hot(iota((ROWS8, EXPERTS), 0) // PACKED == iota((ROWS8, EXPERTS), 1)).astype(BF16)
    member8 = product(widen, member)
    rank8 = jnp.where(member8 > 0.5, product(widen, rank), -1.0)
    weight8 = product(widen, weight.astype(BF16))
    place = iota((ROWS8, TOK), 0) % PACKED
    own = one_hot((rank8 == place.astype(F32)) & (place < CAP))
    combine_ref[0] = own.T.astype(BF16)
    for g in range(3):
        goal = (place - CAP) * 3 + g
        tail = one_hot((rank8 == goal.astype(F32)) & (place >= CAP))
        combine_ref[g + 1] = tail.T.astype(BF16)
        left_ref[g] = jnp.concatenate([own, tail], axis=1).astype(BF16)
    prob = jnp.sum(own * weight8, axis=1, keepdims=True)
    row = iota((ROWS8, 128), 0)
    diagonal = jnp.where(row % PACKED == iota((ROWS8, 128), 1), prob, 0.0).astype(BF16)
    r = iota((ROWS8, ROWS8), 0)
    c = iota((ROWS8, ROWS8), 1)
    lift = one_hot((r // PACKED == c // PACKED) & (r % PACKED == CAP)).astype(BF16)
    spare_ref[...] = product(lift, diagonal).astype(BF16)


def spread(left_ref, x_ref, out_ref):
    rest = x_ref[:, WIDE:]
    for g in range(3):
        cols = pl.ds(g * TAIL, TAIL)
        right = jnp.concatenate([x_ref[:, cols], rest], axis=0)
        out_ref[:, cols] = product(left_ref[g], right).astype(BF16)
    return product(left_ref[0][:, :TOK], x_ref[:, 3 * TAIL : WIDE])


def spread_x_kernel(ids_ref, probs_ref, x_ref, out_ref, left_ref, combine_ref, spare_ref):
    @pl.when(pl.program_id(0) == 0)
    def _():
        tables(ids_ref[...], probs_ref[...], left_ref, combine_ref, spare_ref)

    out_ref[:, 3 * TAIL :] = spread(left_ref, x_ref, out_ref).astype(BF16)


def spread_dy_kernel(left_ref, spare_ref, x_ref, out_ref):
    last = spread(left_ref, x_ref, out_ref)
    out_ref[:, 3 * TAIL :] = last.astype(BF16) + spare_ref[...]


def unpack_masks(main_ref, tail_ref):
    r = iota((SLOTS, ROWS8), 0)
    c = iota((SLOTS, ROWS8), 1)
    same = r // CAP == c // PACKED
    slot = r % CAP
    place = c % PACKED
    main_ref[...] = one_hot(same & (slot == place)).astype(BF16)
    for g in range(3):
        tail = one_hot(same & (place >= CAP) & (slot == (place - CAP) * 3 + g))
        tail_ref[:, g * ROWS8 : (g + 1) * ROWS8] = tail.astype(BF16)


def stacked(packed):
    return jnp.concatenate([packed[:, g * TAIL : (g + 1) * TAIL] for g in range(3)], axis=0)


def unpack(main_ref, tail_ref, packed, rows_ref):
    rows_ref[:, :WIDE] = product(main_ref[...], packed).astype(BF16)
    rows_ref[:, WIDE:] = product(tail_ref[...], stacked(packed)).astype(BF16)


def unpack_all(packed_ref, rows_ref, main_ref, tail_ref):
    unpack_masks(main_ref, tail_ref)
    for j in range(packed_ref.shape[0] // ROWS8):
        rows = rows_ref.at[pl.ds(j * SLOTS, SLOTS)]
        unpack(main_ref, tail_ref, packed_ref[pl.ds(j * ROWS8, ROWS8), :], rows)


def gate_up_kernel(packed_ref, gate_ref, up_ref, rows_ref, parts_ref, main_ref, tail_ref):
    unpack_all(packed_ref, rows_ref, main_ref, tail_ref)
    hidden = gate_ref.shape[1]

    @pl.loop(0, hidden, step=256)
    def _(c):
        rows = rows_ref[...]
        c = pl.multiple_of(c, 256)
        cols = pl.ds(c, 256)
        parts_ref[:, cols] = product(rows, gate_ref[:, cols]).astype(BF16)
        later = pl.ds(pl.multiple_of(hidden + c, 256), 256)
        parts_ref[:, later] = product(rows, up_ref[:, cols]).astype(BF16)


def back_kernel(packed_ref, down_ref, rows_ref, part_ref, prob_ref, main_ref, tail_ref):
    unpack_all(packed_ref, rows_ref, main_ref, tail_ref)
    r = iota((SLOTS, ROWS8), 0)
    c = iota((SLOTS, ROWS8), 1)
    pick = one_hot((r // CAP == c // PACKED) & (c % PACKED == CAP)).astype(BF16)
    mine = iota((SLOTS, 128), 0) % CAP == iota((SLOTS, 128), 1)
    for j in range(packed_ref.shape[0] // ROWS8):
        probs = product(pick, packed_ref[pl.ds(j * ROWS8, ROWS8), 3 * TAIL :])
        prob = jnp.sum(jnp.where(mine, probs, 0.0), axis=1, keepdims=True)
        prob_ref[pl.ds(j * SLOTS, SLOTS), :] = jnp.broadcast_to(prob, (SLOTS, 128)).astype(BF16)

    @pl.loop(0, down_ref.shape[1], step=256)
    def _(c):
        cols = pl.ds(pl.multiple_of(c, 256), 256)
        part_ref[:, cols] = product(rows_ref[...], down_ref[:, cols]).astype(BF16)


def activate_kernel(
    gate_up_ref, back_ref, prob_ref, first_ref, second_ref, weighted_ref, slot_ref
):
    hidden = back_ref.shape[1]
    half = first_ref.shape[0]
    step = 32
    for start in range(0, back_ref.shape[0], step):
        rows = pl.ds(start, step)
        grads_ref = first_ref if start < half else second_ref
        at = pl.ds(start % half, step)
        gate = gate_up_ref[rows, :hidden].astype(F32)
        up = gate_up_ref[rows, hidden:].astype(F32)
        back = back_ref[rows, :].astype(F32)
        weight = prob_ref[rows, :1].astype(F32)
        sigmoid = 1.0 / (1.0 + jnp.exp(-gate))
        swish = gate * sigmoid
        act = swish * up
        grad_act = weight * back
        grad_gate = grad_act * up * sigmoid * (1.0 + gate * (1.0 - sigmoid))
        grads_ref[at, :hidden] = grad_gate.astype(BF16)
        grads_ref[at, hidden:] = (grad_act * swish).astype(BF16)
        weighted_ref[rows, :] = (weight * act).astype(BF16)
        slot = jnp.sum(back * act, axis=1, keepdims=True)
        mine = (start + iota((step, 128), 0)) % CAP == iota((step, 128), 1)
        slot_ref[rows, :] = jnp.where(mine, slot, 0.0).astype(BF16)


def pack(rows_t, out_ref):
    r = iota((ROWS8, SLOTS), 0)
    c = iota((ROWS8, SLOTS), 1)
    same = r // PACKED == c // CAP
    place = r % PACKED
    slot = c % CAP
    main = one_hot(same & (slot == place)).astype(BF16)
    rest = rows_t[WIDE:]
    for g in range(3):
        tail = one_hot(same & (place >= CAP) & (slot == (place - CAP) * 3 + g)).astype(BF16)
        left = jnp.concatenate([main, tail], axis=1)
        right = jnp.concatenate([rows_t[g * TAIL : (g + 1) * TAIL], rest], axis=1)
        out_ref[:, g * TAIL : (g + 1) * TAIL] = product_t(left, right).astype(BF16)
    return product_t(main, rows_t[3 * TAIL : WIDE])


def row_grads(first_ref, second_ref, gate_ref, up_ref):
    hidden = gate_ref.shape[1]
    grads = jnp.concatenate([first_ref[...], second_ref[...]], axis=0)
    rows = product_t(gate_ref[...], grads[:, :hidden])
    return (rows + product_t(up_ref[...], grads[:, hidden:])).astype(BF16)


def row_grad_own_kernel(where_ref, first_ref, second_ref, gate_ref, up_ref, slot_ref, out_ref):
    last = pack(row_grads(first_ref, second_ref, gate_ref, up_ref), out_ref)
    r = iota((ROWS8, SLOTS), 0)
    c = iota((ROWS8, SLOTS), 1)
    lift = one_hot((r // PACKED == c // CAP) & (r % PACKED == CAP)).astype(BF16)
    out_ref[:, 3 * TAIL :] = (last + product(lift, slot_ref[...])).astype(BF16)


def row_grad_kernel(where_ref, first_ref, second_ref, gate_ref, up_ref, before_ref, out_ref):
    last = pack(row_grads(first_ref, second_ref, gate_ref, up_ref), out_ref)
    out_ref[:, 3 * TAIL :] = last.astype(BF16)


def combine_kernel(ids_ref, left_ref, combine_ref, packed_ref, out_ref, probs_ref, slot_ref):
    step = pl.program_id(0)
    packed = packed_ref[...]
    out_ref[:, :WIDE] = product(combine_ref[0], packed).astype(BF16)
    tails = jnp.concatenate([combine_ref[g + 1] for g in range(3)], axis=1)
    out_ref[:, WIDE:] = product(tails, stacked(packed)).astype(BF16)
    spare = packed[:, 3 * TAIL :].astype(F32)

    @pl.when(step == 0)
    def _():
        slot_ref[...] = spare

    @pl.when(step > 0)
    def _():
        slot_ref[...] += spare

    @pl.when(step == pl.num_programs(0) - 1)
    def _():
        row = iota((ROWS8, 128), 0)
        slots = jnp.where(row % PACKED == CAP, slot_ref[...], 0.0).astype(BF16)
        r = iota((ROWS8, ROWS8), 0)
        c = iota((ROWS8, ROWS8), 1)
        group = one_hot(r // PACKED == c // PACKED).astype(BF16)
        wide = product(group, slots)
        mine = iota((ROWS8, 128), 1) == row % PACKED
        column = jnp.sum(jnp.where(mine, wide, 0.0), axis=1, keepdims=True)
        value = (left_ref[0, :, :TOK].astype(F32) * column).astype(BF16)
        gather = one_hot(iota((EXPERTS, ROWS8), 1) // PACKED == iota((EXPERTS, ROWS8), 0))
        table = product(gather.astype(BF16), value)
        expert = iota((EXPERTS, TOK), 0)
        for k in range(TOP):
            hit = ids_ref[k : k + 1, :] == expert
            found = jnp.sum(jnp.where(hit, table, 0.0), axis=0, keepdims=True)
            probs_ref[k : k + 1, :] = found


def call(kernel, grid, ins, outs, scratch=(), flops=0, moved=0, prefetch=0, aliases=None):
    return pl.pallas_call(
        kernel,
        grid_spec=pltpu.PrefetchScalarGridSpec(
            num_scalar_prefetch=prefetch,
            grid=(grid,),
            in_specs=ins,
            out_specs=[s for s, _, _ in outs],
            scratch_shapes=list(scratch),
        ),
        out_shape=[place(shape, kind) for _, (shape, kind), place in outs],
        compiler_params=pltpu.CompilerParams(
            dimension_semantics=("arbitrary",), vmem_limit_bytes=24 * MIB
        ),
        input_output_aliases=aliases or {},
        cost_estimate=pl.CostEstimate(flops=flops, bytes_accessed=moved, transcendentals=0),
    )


def whole(*shape):
    return pl.BlockSpec(shape, lambda *i: (0,) * len(shape))


def rows_of(rows, cols):
    return pl.BlockSpec((rows, cols), lambda i, *_: (i, 0))


def cols_of(rows, cols):
    return pl.BlockSpec((rows, cols), lambda i, *_: (0, i))


NEAR = pl.BlockSpec(memory_space=pltpu.VMEM)


def on_device(hidden_in, grad_out, route_ids, route_probs, w_gate, w_up, w_down):
    sp_count = lax.axis_size("sp")
    pieces = lax.axis_size("ep") * sp_count
    hidden = w_gate.shape[2]
    model = hidden_in.shape[1]
    all_rows = pieces * CAP
    packed8 = pieces * PACKED
    gate_weight, up_weight, down_weight = w_gate[0], w_up[0], w_down[0]
    ids, probs = route_ids.T, route_probs.T
    far, near = pltpu.HBM, jax.ShapeDtypeStruct
    tie = lax.optimization_barrier
    packet = (rows_of(ROWS8, WIDE), ((packed8, WIDE), BF16), far)
    x_send, left, combine, spare = call(
        spread_x_kernel,
        sp_count,
        [whole(TOP, TOK), whole(TOP, TOK), cols_of(TOK, QUARTER)],
        [
            packet,
            (whole(3, ROWS8, ROWS8), ((3, ROWS8, ROWS8), BF16), far),
            (whole(4, TOK, ROWS8), ((4, TOK, ROWS8), BF16), far),
            (whole(ROWS8, 128), ((ROWS8, 128), BF16), far),
        ],
        flops=2 * packed8 * WIDE * 256,
        moved=2 * (packed8 * WIDE + TOK * model),
    )(ids, probs, hidden_in)
    (dy_send,) = call(
        spread_dy_kernel,
        sp_count,
        [whole(3, ROWS8, ROWS8), whole(ROWS8, 128), cols_of(TOK, QUARTER)],
        [packet],
        flops=2 * packed8 * WIDE * 256,
        moved=2 * (packed8 * WIDE + TOK * model),
    )(left, spare, grad_out)

    def exchange(packed):
        pieced = packed.reshape(pieces, PACKED, WIDE)
        moved = lax.all_to_all(pieced, ("sp", "ep"), split_axis=0, concat_axis=0, tiled=True)
        return moved.reshape(packed8, WIDE)

    x_packed = exchange(x_send)
    x_packed, dy_send, down_turned = tie((x_packed, dy_send, tie(down_weight.T)))
    dy_packed = exchange(dy_send)
    masks = (pltpu.VMEM((SLOTS, ROWS8), BF16), pltpu.VMEM((SLOTS, 3 * ROWS8), BF16))
    rows_out = (whole(all_rows, QUARTER), ((all_rows, QUARTER), BF16), far)
    x_rows, gate_up_part = call(
        gate_up_kernel,
        1,
        [NEAR, NEAR, NEAR],
        [rows_out, (whole(all_rows, 2 * hidden), ((all_rows, 2 * hidden), BF16), far)],
        masks,
        flops=4 * all_rows * QUARTER * hidden,
        moved=2 * (packed8 * WIDE + 2 * QUARTER * hidden + all_rows * (QUARTER + 2 * hidden)),
    )(x_packed, gate_weight, up_weight)
    gate_up = lax.psum_scatter(gate_up_part, "sp", scatter_dimension=0, tiled=True)
    dy_packed, _ = tie((dy_packed, gate_up_part))
    dy_rows, back_part, prob_rows = call(
        back_kernel,
        1,
        [NEAR, NEAR],
        [
            rows_out,
            (whole(all_rows, hidden), ((all_rows, hidden), BF16), far),
            (whole(all_rows, 128), ((all_rows, 128), BF16), far),
        ],
        masks,
        flops=32 * 2 * all_rows * QUARTER * hidden,
        moved=2 * (packed8 * WIDE + QUARTER * hidden + all_rows * (QUARTER + hidden)),
    )(dy_packed, down_turned)
    back_part, gate_up = tie((back_part, gate_up))
    back = lax.psum_scatter(back_part, "sp", scatter_dimension=0, tiled=True)
    own = lax.axis_index("sp").astype(jnp.int32)
    own_rows = all_rows // sp_count
    half = own_rows // 2
    prob_own = lax.dynamic_slice_in_dim(prob_rows, own * own_rows, own_rows, axis=0)
    first, second, weighted_own, slot_own = call(
        activate_kernel,
        1,
        [NEAR, NEAR, NEAR],
        [
            (whole(half, 2 * hidden), ((half, 2 * hidden), BF16), far),
            (whole(half, 2 * hidden), ((half, 2 * hidden), BF16), far),
            (whole(own_rows, hidden), ((own_rows, hidden), BF16), far),
            (whole(own_rows, 128), ((own_rows, 128), BF16), near),
        ],
        flops=20 * own_rows * hidden,
        moved=12 * own_rows * hidden,
    )(gate_up, back, prob_own)
    upward = [(i, (i + 1) % sp_count) for i in range(sp_count)]
    downward = [(i, (i - 1) % sp_count) for i in range(sp_count)]
    below_first = lax.ppermute(first, "sp", upward)
    above_second = lax.ppermute(second, "sp", downward)
    below_second = lax.ppermute(second, "sp", upward)
    above_first = lax.ppermute(first, "sp", downward)
    landing = (
        pl.BlockSpec((ROWS8, WIDE), lambda i, at: (at[0], 0)),
        ((packed8, WIDE), BF16),
        far,
    )
    row_cost = dict(
        flops=4 * own_rows * QUARTER * hidden,
        moved=2 * (ROWS8 * WIDE + 2 * QUARTER * hidden + own_rows * 2 * hidden),
        prefetch=1,
    )
    (back_send,) = call(
        row_grad_own_kernel, 1, [NEAR, NEAR, NEAR, NEAR, NEAR], [landing], **row_cost
    )(own.reshape(1), first, second, gate_weight, up_weight, slot_own)

    def row_grad(at, halves, back_send):
        return call(
            row_grad_kernel,
            1,
            [NEAR, NEAR, NEAR, NEAR, pl.BlockSpec(memory_space=pl.ANY)],
            [landing],
            aliases={5: 0},
            **row_cost,
        )(at.reshape(1), *halves, gate_weight, up_weight, back_send)[0]

    below_first, above_second, back_send = tie((below_first, above_second, back_send))
    across_first = lax.ppermute(below_first, "sp", upward)
    across_second = lax.ppermute(above_second, "sp", downward)
    below, above, across = ((own + n) % sp_count for n in (sp_count - 1, 1, 2))
    back_send = row_grad(below, (below_first, below_second), back_send)
    back_send = row_grad(above, (above_first, above_second), back_send)
    across_first, across_second, back_send = tie((across_first, across_second, back_send))
    weighted_own, _, _ = tie((weighted_own, across_first, across_second))
    weighted = lax.all_gather(weighted_own, "sp", axis=0, tiled=True)
    back_send = row_grad(across, (across_first, across_second), back_send)
    back_packed = exchange(back_send)
    pieces_of = (
        (own, 0, first),
        (own, half, second),
        (below, 0, below_first),
        (below, half, below_second),
        (above, 0, above_first),
        (above, half, above_second),
        (across, 0, across_first),
        (across, half, across_second),
    )
    grads_all = jnp.zeros((all_rows, 2 * hidden), BF16)
    grads_all, _ = tie((grads_all, back_send))
    for at, shift, grads in pieces_of:
        grads_all = lax.dynamic_update_slice_in_dim(
            grads_all, grads, at * own_rows + shift, axis=0
        )
    contract_rows = (((0,), (0,)), ((), ()))

    def over_rows(a, b):
        return lax.dot_general(a, b, contract_rows, preferred_element_type=F32).astype(BF16)

    grad_gate_weight = over_rows(x_rows, grads_all[:, :hidden])
    grad_up_weight = over_rows(x_rows, grads_all[:, hidden:])
    grad_down_weight = over_rows(weighted, dy_rows)
    grad_in, grad_probs = call(
        combine_kernel,
        sp_count,
        [whole(TOP, TOK), whole(3, ROWS8, ROWS8), whole(4, TOK, ROWS8), rows_of(ROWS8, WIDE)],
        [
            (cols_of(TOK, QUARTER), ((TOK, model), BF16), near),
            (whole(TOP, TOK), ((TOP, TOK), F32), near),
        ],
        (pltpu.VMEM((ROWS8, 128), F32),),
        flops=2 * packed8 * WIDE * TOK * 2,
        moved=2 * (packed8 * WIDE + TOK * model),
    )(ids, left, combine, back_packed)
    return (
        grad_in,
        grad_gate_weight[None],
        grad_up_weight[None],
        grad_down_weight[None],
        grad_probs.astype(BF16).T,
    )


def solution(mesh):
    placed = (
        P(("ep", "sp"), None),
        P(("ep", "sp"), None),
        P(("ep", "sp"), None),
        P(("ep", "sp"), None),
        P("ep", "sp", None),
        P("ep", "sp", None),
        P("ep", None, "sp"),
    )
    return jax.shard_map(
        on_device,
        mesh=mesh,
        in_specs=placed,
        out_specs=(
            P(("ep", "sp"), None),
            P("ep", "sp", None),
            P("ep", "sp", None),
            P("ep", None, "sp"),
            P(("ep", "sp"), None),
        ),
        check_vma=False,
    )
```

```python
import functools

import jax
import jax.numpy as jnp
from jax import lax
from jax.experimental import pallas as pl
from jax.experimental.pallas import tpu as pltpu
from jax.sharding import PartitionSpec as P

CAP = 6
EXPERTS = 32
TOK = 128
TOP = 8
WIDE = 1280
TAIL = 384
QUARTER = WIDE + TAIL
PACKED = 8
BLOCK = 32
SLOTS = BLOCK * CAP
ROWS8 = BLOCK * PACKED
MIB = 1 << 20
BF16 = jnp.bfloat16
F32 = jnp.float32


def iota(shape, dim):
    return lax.broadcasted_iota(jnp.int32, shape, dim)


def product(a, b):
    return jnp.dot(a, b, preferred_element_type=F32)


def product_t(a, b):
    return lax.dot_general(a, b, (((1,), (1,)), ((), ())), preferred_element_type=F32)


def one_hot(mask):
    return jnp.where(mask, 1.0, 0.0)


def tables(ids, probs, left_ref, combine_ref, spare_ref):
    expert = iota((EXPERTS, TOK), 0)
    member = jnp.zeros((EXPERTS, TOK), F32)
    weight = jnp.zeros((EXPERTS, TOK), F32)
    for k in range(TOP):
        hit = ids[k : k + 1, :] == expert
        member = member + jnp.where(hit, 1.0, 0.0)
        weight = weight + jnp.where(hit, probs[k : k + 1, :], 0.0)
    member = member.astype(BF16)
    before = one_hot(iota((TOK, TOK), 0) < iota((TOK, TOK), 1)).astype(BF16)
    rank = product(member, before).astype(BF16)
    widen = one_hot(iota((ROWS8, EXPERTS), 0) // PACKED == iota((ROWS8, EXPERTS), 1)).astype(BF16)
    member8 = product(widen, member)
    rank8 = jnp.where(member8 > 0.5, product(widen, rank), -1.0)
    weight8 = product(widen, weight.astype(BF16))
    place = iota((ROWS8, TOK), 0) % PACKED
    own = one_hot((rank8 == place.astype(F32)) & (place < CAP))
    combine_ref[0] = own.T.astype(BF16)
    for g in range(3):
        goal = (place - CAP) * 3 + g
        tail = one_hot((rank8 == goal.astype(F32)) & (place >= CAP))
        combine_ref[g + 1] = tail.T.astype(BF16)
        left_ref[g] = jnp.concatenate([own, tail], axis=1).astype(BF16)
    prob = jnp.sum(own * weight8, axis=1, keepdims=True)
    row = iota((ROWS8, 128), 0)
    diagonal = jnp.where(row % PACKED == iota((ROWS8, 128), 1), prob, 0.0).astype(BF16)
    r = iota((ROWS8, ROWS8), 0)
    c = iota((ROWS8, ROWS8), 1)
    lift = one_hot((r // PACKED == c // PACKED) & (r % PACKED == CAP)).astype(BF16)
    spare_ref[...] = product(lift, diagonal).astype(BF16)


def spread(left_ref, x_ref, out_ref):
    rest = x_ref[:, WIDE:]
    for g in range(3):
        cols = pl.ds(g * TAIL, TAIL)
        right = jnp.concatenate([x_ref[:, cols], rest], axis=0)
        out_ref[:, cols] = product(left_ref[g], right).astype(BF16)
    return product(left_ref[0][:, :TOK], x_ref[:, 3 * TAIL : WIDE])


def spread_x_kernel(ids_ref, probs_ref, x_ref, out_ref, left_ref, combine_ref, spare_ref):
    @pl.when(pl.program_id(0) == 0)
    def _():
        tables(ids_ref[...], probs_ref[...], left_ref, combine_ref, spare_ref)

    out_ref[:, 3 * TAIL :] = spread(left_ref, x_ref, out_ref).astype(BF16)


def spread_dy_kernel(left_ref, spare_ref, x_ref, out_ref):
    last = spread(left_ref, x_ref, out_ref)
    out_ref[:, 3 * TAIL :] = last.astype(BF16) + spare_ref[...]


def unpack_masks(main_ref, tail_ref):
    r = iota((SLOTS, ROWS8), 0)
    c = iota((SLOTS, ROWS8), 1)
    same = r // CAP == c // PACKED
    slot = r % CAP
    place = c % PACKED
    main_ref[...] = one_hot(same & (slot == place)).astype(BF16)
    for g in range(3):
        tail = one_hot(same & (place >= CAP) & (slot == (place - CAP) * 3 + g))
        tail_ref[:, g * ROWS8 : (g + 1) * ROWS8] = tail.astype(BF16)


def stacked(packed):
    return jnp.concatenate([packed[:, g * TAIL : (g + 1) * TAIL] for g in range(3)], axis=0)


def unpack(main_ref, tail_ref, packed, rows_ref):
    rows_ref[:, :WIDE] = product(main_ref[...], packed).astype(BF16)
    rows_ref[:, WIDE:] = product(tail_ref[...], stacked(packed)).astype(BF16)


def unpack_all(packed_ref, rows_ref, main_ref, tail_ref):
    for j in range(packed_ref.shape[0] // ROWS8):
        rows = rows_ref.at[pl.ds(j * SLOTS, SLOTS)]
        unpack(main_ref, tail_ref, packed_ref[pl.ds(j * ROWS8, ROWS8), :], rows)


def shares(source, held, sems):
    count = sems.shape[0]
    rows = held.shape[0] // count
    parts = [pl.ds(i * rows, rows) for i in range(count)]
    return [
        pltpu.make_async_copy(source.at[part], held.at[part], sems.at[i])
        for i, part in enumerate(parts)
    ]


def start(copies):
    for copy in copies:
        copy.start()


def finish(copies):
    for copy in copies:
        copy.wait()


def gate_up_kernel(
    packed_ref, gate_hbm, up_hbm, rows_ref, parts_ref, gate_ref, up_ref, gate_sem, up_sem, *masks
):
    first = pl.program_id(0) == 0
    weights = ((gate_hbm, gate_ref, gate_sem), (up_hbm, up_ref, up_sem))

    @pl.when(first)
    def _():
        for weight in weights:
            start(shares(*weight))
        unpack_masks(*masks)

    unpack_all(packed_ref, rows_ref, *masks)
    hidden = gate_ref.shape[1]
    for j, weight in enumerate(weights):

        @pl.when(first)
        def _(weight=weight):
            finish(shares(*weight))

        cols = pl.ds(j * hidden, hidden)
        parts_ref[:, cols] = product(rows_ref[...], weight[1][...]).astype(BF16)


def block_of(rows_ref, at, count=SLOTS):
    return rows_ref[pl.ds(pl.multiple_of(at * SLOTS, SLOTS), count), :]


def back_far_kernel(
    at_ref, packed_ref, down_hbm, rows_ref, first_ref, second_ref, prob_ref, down_ref, sem, *masks
):
    copies = shares(down_hbm, down_ref, sem)
    start(copies)
    unpack_masks(*masks)
    unpack_all(packed_ref, rows_ref, *masks)
    finish(copies)
    part = product_t(block_of(rows_ref, at_ref[3]), down_ref[...]).astype(BF16)
    half = first_ref.shape[0]
    first_ref[...] = part[:half]
    second_ref[...] = part[half:]
    r = iota((SLOTS, ROWS8), 0)
    c = iota((SLOTS, ROWS8), 1)
    pick = one_hot((r // CAP == c // PACKED) & (c % PACKED == CAP)).astype(BF16)
    mine = iota((SLOTS, 128), 0) % CAP == iota((SLOTS, 128), 1)
    own8 = pl.ds(pl.multiple_of(at_ref[0] * ROWS8, ROWS8), ROWS8)
    probs = product(pick, packed_ref[own8, 3 * TAIL :])
    prob = jnp.sum(jnp.where(mine, probs, 0.0), axis=1, keepdims=True)
    prob_ref[...] = jnp.broadcast_to(prob, (SLOTS, 128)).astype(BF16)


def back_near_kernel(at_ref, rows_ref, down_hbm, own_ref, below_ref, above_ref, down_ref, sem):
    copies = shares(down_hbm, down_ref, sem)
    start(copies)
    finish(copies)
    blocks = [block_of(rows_ref, at_ref[j]) for j in range(3)]
    part = product_t(jnp.concatenate(blocks, axis=0), down_ref[...]).astype(BF16)
    own_ref[...] = part[:SLOTS]
    below_ref[...] = part[SLOTS : 2 * SLOTS]
    above_ref[...] = part[2 * SLOTS :]


def join_kernel(below_ref, above_ref, first_ref, second_ref, below_out, above_out):
    half = first_ref.shape[0]
    below_out[:half] = below_ref[:half]
    below_out[half:] = (below_ref[half:].astype(F32) + second_ref[...].astype(F32)).astype(BF16)
    above_out[:half] = (above_ref[:half].astype(F32) + first_ref[...].astype(F32)).astype(BF16)
    above_out[half:] = above_ref[half:]


def activate_kernel(
    gate_up_ref, own_ref, left_ref, right_ref, prob_ref, first_ref, second_ref, weighted_ref, slot_ref
):
    rows, hidden = own_ref.shape
    half = first_ref.shape[0]
    step = 32
    for start in range(0, rows, step):
        at = pl.ds(start, step)
        grads_ref = first_ref if start < half else second_ref
        to = pl.ds(start % half, step)
        gate = gate_up_ref[at, :hidden].astype(F32)
        up = gate_up_ref[at, hidden:].astype(F32)
        back = own_ref[at, :].astype(F32) + left_ref[at, :].astype(F32)
        back = back + right_ref[at, :].astype(F32)
        weight = prob_ref[at, :1].astype(F32)
        sigmoid = 1.0 / (1.0 + jnp.exp(-gate))
        swish = gate * sigmoid
        act = swish * up
        grad_act = weight * back
        grad_gate = grad_act * up * sigmoid * (1.0 + gate * (1.0 - sigmoid))
        grads_ref[to, :hidden] = grad_gate.astype(BF16)
        grads_ref[to, hidden:] = (grad_act * swish).astype(BF16)
        weighted_ref[at, :] = (weight * act).astype(BF16)
        slot = jnp.sum(back * act, axis=1, keepdims=True)
        mine = (start + iota((step, 128), 0)) % CAP == iota((step, 128), 1)
        slot_ref[at, :] = jnp.where(mine, slot, 0.0).astype(BF16)


def pack(rows, out_ref):
    r = iota((ROWS8, SLOTS), 0)
    c = iota((ROWS8, SLOTS), 1)
    same = r // PACKED == c // CAP
    place = r % PACKED
    slot = c % CAP
    main = one_hot(same & (slot == place)).astype(BF16)
    rest = rows[:, WIDE:]
    for g in range(3):
        tail = one_hot(same & (place >= CAP) & (slot == (place - CAP) * 3 + g)).astype(BF16)
        left = jnp.concatenate([main, tail], axis=1)
        right = jnp.concatenate([rows[:, g * TAIL : (g + 1) * TAIL], rest], axis=0)
        out_ref[:, g * TAIL : (g + 1) * TAIL] = product(left, right).astype(BF16)
    return product(main, rows[:, 3 * TAIL : WIDE])


def row_grad_kernel(blocks, own, at_ref, *refs):
    grads_refs, rest = refs[:-9], refs[-9:]
    gate_hbm, up_hbm, extra_ref, out_ref, rows_ref, gate_ref, up_ref, gate_sem, up_sem = rest
    hidden = gate_ref.shape[1]
    step = pl.program_id(0)

    @pl.when(step == 0)
    def _():
        gate_copies = shares(gate_hbm, gate_ref, gate_sem)
        up_copies = shares(up_hbm, up_ref, up_sem)
        start(gate_copies)
        start(up_copies)
        grads = jnp.concatenate([r[...] for r in grads_refs], axis=0)
        finish(gate_copies)
        rows = product_t(grads[:, :hidden], gate_ref[...])
        finish(up_copies)
        rows_ref[...] = (rows + product_t(grads[:, hidden:], up_ref[...])).astype(BF16)

    for j in range(blocks):

        @pl.when(step == j)
        def _(j=j):
            spare = pack(rows_ref[j * SLOTS : (j + 1) * SLOTS, :], out_ref)
            if own:
                r = iota((ROWS8, SLOTS), 0)
                c = iota((ROWS8, SLOTS), 1)
                lift = one_hot((r // PACKED == c // CAP) & (r % PACKED == CAP)).astype(BF16)
                spare = spare + product(lift, extra_ref[...])
            out_ref[:, 3 * TAIL :] = spare.astype(BF16)


def combine_kernel(ids_ref, left_ref, combine_ref, packed_ref, out_ref, probs_ref, slot_ref):
    step = pl.program_id(0)
    packed = packed_ref[...]
    out_ref[:, :WIDE] = product(combine_ref[0], packed).astype(BF16)
    tails = jnp.concatenate([combine_ref[g + 1] for g in range(3)], axis=1)
    out_ref[:, WIDE:] = product(tails, stacked(packed)).astype(BF16)
    spare = packed[:, 3 * TAIL :].astype(F32)

    @pl.when(step == 0)
    def _():
        slot_ref[...] = spare

    @pl.when(step > 0)
    def _():
        slot_ref[...] += spare

    @pl.when(step == pl.num_programs(0) - 1)
    def _():
        row = iota((ROWS8, 128), 0)
        slots = jnp.where(row % PACKED == CAP, slot_ref[...], 0.0).astype(BF16)
        r = iota((ROWS8, ROWS8), 0)
        c = iota((ROWS8, ROWS8), 1)
        group = one_hot(r // PACKED == c // PACKED).astype(BF16)
        wide = product(group, slots)
        mine = iota((ROWS8, 128), 1) == row % PACKED
        column = jnp.sum(jnp.where(mine, wide, 0.0), axis=1, keepdims=True)
        value = (left_ref[0, :, :TOK].astype(F32) * column).astype(BF16)
        gather = one_hot(iota((EXPERTS, ROWS8), 1) // PACKED == iota((EXPERTS, ROWS8), 0))
        table = product(gather.astype(BF16), value)
        expert = iota((EXPERTS, TOK), 0)
        for k in range(TOP):
            hit = ids_ref[k : k + 1, :] == expert
            found = jnp.sum(jnp.where(hit, table, 0.0), axis=0, keepdims=True)
            probs_ref[k : k + 1, :] = found


def call(
    kernel, grid, ins, outs, scratch=(), flops=0, moved=0, prefetch=0, aliases=None, limit=24
):
    return pl.pallas_call(
        kernel,
        grid_spec=pltpu.PrefetchScalarGridSpec(
            num_scalar_prefetch=prefetch,
            grid=(grid,),
            in_specs=ins,
            out_specs=[s for s, _, _ in outs],
            scratch_shapes=list(scratch),
        ),
        out_shape=[place(shape, kind) for _, (shape, kind), place in outs],
        compiler_params=pltpu.CompilerParams(
            dimension_semantics=("arbitrary",), vmem_limit_bytes=limit * MIB
        ),
        input_output_aliases=aliases or {},
        cost_estimate=pl.CostEstimate(flops=flops, bytes_accessed=moved, transcendentals=0),
    )


def whole(*shape):
    return pl.BlockSpec(shape, lambda *i: (0,) * len(shape))


def rows_of(rows, cols):
    return pl.BlockSpec((rows, cols), lambda i, *_: (i, 0))


def cols_of(rows, cols):
    return pl.BlockSpec((rows, cols), lambda i, *_: (0, i))


ANY = pl.BlockSpec(memory_space=pl.ANY)


def on_device(hidden_in, grad_out, route_ids, route_probs, w_gate, w_up, w_down):
    sp_count = lax.axis_size("sp")
    pieces = lax.axis_size("ep") * sp_count
    hidden = w_gate.shape[2]
    model = hidden_in.shape[1]
    all_rows = pieces * CAP
    packed8 = pieces * PACKED
    gate_weight, up_weight, down_weight = w_gate[0], w_up[0], w_down[0]
    ids, probs = route_ids.T, route_probs.T

    def in_hbm(array):
        return pltpu.with_memory_space_constraint(array, pltpu.HBM)

    hidden_in, grad_out = in_hbm(hidden_in), in_hbm(grad_out)
    far, near = pltpu.HBM, jax.ShapeDtypeStruct
    tie = lax.optimization_barrier
    packet = (rows_of(ROWS8, WIDE), ((packed8, WIDE), BF16), far)
    x_send, left, combine, spare = call(
        spread_x_kernel,
        sp_count,
        [whole(TOP, TOK), whole(TOP, TOK), cols_of(TOK, QUARTER)],
        [
            packet,
            (whole(3, ROWS8, ROWS8), ((3, ROWS8, ROWS8), BF16), far),
            (whole(4, TOK, ROWS8), ((4, TOK, ROWS8), BF16), far),
            (whole(ROWS8, 128), ((ROWS8, 128), BF16), far),
        ],
        flops=2 * packed8 * WIDE * 256,
        moved=2 * (packed8 * WIDE + TOK * model),
    )(in_hbm(ids), in_hbm(probs), hidden_in)
    (dy_send,) = call(
        spread_dy_kernel,
        sp_count,
        [whole(3, ROWS8, ROWS8), whole(ROWS8, 128), cols_of(TOK, QUARTER)],
        [packet],
        flops=2 * packed8 * WIDE * 256,
        moved=2 * (packed8 * WIDE + TOK * model),
    )(in_hbm(left), in_hbm(spare), grad_out)

    def exchange(packed):
        pieced = packed.reshape(pieces, PACKED, WIDE)
        moved = lax.all_to_all(pieced, ("sp", "ep"), split_axis=0, concat_axis=0, tiled=True)
        return moved.reshape(packed8, WIDE)

    gate_weight, up_weight, down_weight = map(in_hbm, (gate_weight, up_weight, down_weight))
    x_packed = exchange(x_send)
    x_packed, dy_send = tie((in_hbm(x_packed), dy_send))
    dy_packed = exchange(dy_send)
    masks = (pltpu.VMEM((SLOTS, ROWS8), BF16), pltpu.VMEM((SLOTS, 3 * ROWS8), BF16))
    two_weights = (pltpu.VMEM((QUARTER, hidden), BF16),) * 2 + (pltpu.SemaphoreType.DMA((4,)),) * 2
    down_space = (pltpu.VMEM((hidden, QUARTER), BF16), pltpu.SemaphoreType.DMA((4,)))
    some_rows, some8 = all_rows // 2, packed8 // 2
    x_rows, gate_up_part = call(
        gate_up_kernel,
        2,
        [rows_of(some8, WIDE), ANY, ANY],
        [
            (rows_of(some_rows, QUARTER), ((all_rows, QUARTER), BF16), far),
            (rows_of(some_rows, 2 * hidden), ((all_rows, 2 * hidden), BF16), far),
        ],
        two_weights + masks,
        flops=4 * all_rows * QUARTER * hidden,
        moved=2 * (packed8 * WIDE + 2 * QUARTER * hidden + all_rows * (QUARTER + 2 * hidden)),
    )(x_packed, gate_weight, up_weight)
    gate_up = lax.psum_scatter(gate_up_part, "sp", scatter_dimension=0, tiled=True)
    own = lax.axis_index("sp").astype(jnp.int32)
    own_rows = all_rows // sp_count
    half = own_rows // 2
    places = (own + jnp.array([0, sp_count - 1, 1, 2], jnp.int32)) % sp_count
    upward = [(i, (i + 1) % sp_count) for i in range(sp_count)]
    downward = [(i, (i - 1) % sp_count) for i in range(sp_count)]

    def both_ways(up, down):
        return lax.ppermute(up, "sp", upward), lax.ppermute(down, "sp", downward)

    dy_packed, _ = tie((dy_packed, gate_up_part))
    piece = ((half, hidden), BF16)
    block = ((own_rows, hidden), BF16)
    dy_rows, far_first, far_second, prob_own = call(
        back_far_kernel,
        1,
        [whole(packed8, WIDE), ANY],
        [
            (whole(all_rows, QUARTER), ((all_rows, QUARTER), BF16), far),
            (whole(*piece[0]), piece, far),
            (whole(*piece[0]), piece, far),
            (whole(own_rows, 128), ((own_rows, 128), BF16), far),
        ],
        down_space + masks,
        flops=32 * 2 * all_rows * QUARTER * hidden,
        moved=2 * (packed8 * WIDE + QUARTER * hidden + all_rows * QUARTER),
        prefetch=1,
    )(places, dy_packed, down_weight)
    far_first, far_second = both_ways(far_first, far_second)
    back_own, back_below, back_above = call(
        back_near_kernel,
        1,
        [whole(all_rows, QUARTER), ANY],
        [(whole(*block[0]), block, far)] * 3,
        down_space,
        flops=2 * 3 * own_rows * QUARTER * hidden,
        moved=2 * (QUARTER * hidden + all_rows * QUARTER + 3 * own_rows * hidden),
        prefetch=1,
    )(places, in_hbm(dy_rows), down_weight)
    back_below, back_above = call(
        join_kernel,
        1,
        [whole(*block[0])] * 2 + [whole(*piece[0])] * 2,
        [(whole(*block[0]), block, far)] * 2,
        moved=2 * 5 * own_rows * hidden,
    )(in_hbm(back_below), in_hbm(back_above), far_first, far_second)
    left_part, right_part = both_ways(back_above, back_below)
    first, second, weighted_own, slot_own = call(
        activate_kernel,
        1,
        [whole(own_rows, 2 * hidden)] + [whole(*block[0])] * 3 + [whole(own_rows, 128)],
        [
            (whole(half, 2 * hidden), ((half, 2 * hidden), BF16), far),
            (whole(half, 2 * hidden), ((half, 2 * hidden), BF16), far),
            (whole(own_rows, hidden), ((own_rows, hidden), BF16), far),
            (whole(own_rows, 128), ((own_rows, 128), BF16), far),
        ],
        flops=20 * own_rows * hidden,
        moved=12 * own_rows * hidden,
    )(in_hbm(gate_up), in_hbm(back_own), left_part, right_part, in_hbm(prob_own))
    below_first, above_second = both_ways(first, second)
    below_second, above_first = both_ways(second, first)

    def row_grad(shift, grads, extra, own_block=False):
        count = len(grads)
        blocks = count // 2
        landing = pl.BlockSpec((ROWS8, WIDE), lambda i, at: (at[shift + i], 0))
        return call(
            functools.partial(row_grad_kernel, blocks, own_block),
            blocks,
            [whole(half, 2 * hidden)] * count
            + [ANY, ANY, whole(own_rows, 128) if own_block else ANY],
            [(landing, ((packed8, WIDE), BF16), far)],
            (pltpu.VMEM((blocks * SLOTS, QUARTER), BF16), *two_weights),
            aliases={} if own_block else {count + 3: 0},
            flops=4 * blocks * own_rows * QUARTER * hidden,
            moved=2 * (2 * QUARTER * hidden + blocks * (ROWS8 * WIDE + own_rows * 2 * hidden)),
            prefetch=1,
        )(places, *grads, gate_weight, up_weight, extra)[0]

    own_halves = (in_hbm(first), in_hbm(second))
    back_send = row_grad(0, own_halves, in_hbm(slot_own), own_block=True)
    below_first, above_second, back_send = tie((below_first, above_second, back_send))
    across_first, across_second = both_ways(below_first, above_second)
    back_send = row_grad(1, (below_first, below_second, above_first, above_second), back_send)
    across_first, across_second, back_send = tie((across_first, across_second, back_send))
    weighted_own, _, _ = tie((weighted_own, below_second, above_first))
    weighted = lax.all_gather(weighted_own, "sp", axis=0, tiled=True)
    back_send = row_grad(3, (across_first, across_second), back_send)
    back_packed = exchange(back_send)
    below, above, across = (places[j] for j in (1, 2, 3))
    pieces_of = (
        (own, 0, first),
        (own, half, second),
        (below, 0, below_first),
        (below, half, below_second),
        (above, 0, above_first),
        (above, half, above_second),
        (across, 0, across_first),
        (across, half, across_second),
    )
    grads_all = jnp.zeros((all_rows, 2 * hidden), BF16)
    grads_all, _ = tie((grads_all, back_send))
    for at, shift, grads in pieces_of:
        grads_all = lax.dynamic_update_slice_in_dim(
            grads_all, grads, at * own_rows + shift, axis=0
        )
    contract_rows = (((0,), (0,)), ((), ()))

    def over_rows(a, b):
        return lax.dot_general(a, b, contract_rows, preferred_element_type=F32).astype(BF16)

    grad_gate_weight = over_rows(x_rows, grads_all[:, :hidden])
    grad_up_weight = over_rows(x_rows, grads_all[:, hidden:])
    grad_down_weight = over_rows(weighted, dy_rows)
    grad_in, grad_probs = call(
        combine_kernel,
        sp_count,
        [whole(TOP, TOK), whole(3, ROWS8, ROWS8), whole(4, TOK, ROWS8), rows_of(ROWS8, WIDE)],
        [
            (cols_of(TOK, QUARTER), ((TOK, model), BF16), near),
            (whole(TOP, TOK), ((TOP, TOK), F32), near),
        ],
        (pltpu.VMEM((ROWS8, 128), F32),),
        flops=2 * packed8 * WIDE * TOK * 2,
        moved=2 * (packed8 * WIDE + TOK * model),
    )(in_hbm(ids), in_hbm(left), in_hbm(combine), back_packed)
    return (
        grad_in,
        grad_gate_weight[None],
        grad_up_weight[None],
        grad_down_weight[None],
        grad_probs.astype(BF16).T,
    )


def solution(mesh):
    placed = (
        P(("ep", "sp"), None),
        P(("ep", "sp"), None),
        P(("ep", "sp"), None),
        P(("ep", "sp"), None),
        P("ep", "sp", None),
        P("ep", "sp", None),
        P("ep", None, "sp"),
    )
    return jax.shard_map(
        on_device,
        mesh=mesh,
        in_specs=placed,
        out_specs=(
            P(("ep", "sp"), None),
            P("ep", "sp", None),
            P("ep", "sp", None),
            P("ep", None, "sp"),
            P(("ep", "sp"), None),
        ),
        check_vma=False,
    )
```

```python
import functools

import jax
import jax.numpy as jnp
from jax import lax
from jax.experimental import pallas as pl
from jax.experimental.pallas import tpu as pltpu
from jax.sharding import PartitionSpec as P

CAP = 6
EXPERTS = 32
TOK = 128
TOP = 8
WIDE = 1280
TAIL = 384
QUARTER = WIDE + TAIL
PACKED = 8
BLOCK = 32
SLOTS = BLOCK * CAP
ROWS8 = BLOCK * PACKED
RING = 4
MIB = 1 << 20
BF16 = jnp.bfloat16
F32 = jnp.float32


def iota(shape, dim):
    return lax.broadcasted_iota(jnp.int32, shape, dim)


def product(a, b):
    return jnp.dot(a, b, preferred_element_type=F32)


def product_t(a, b):
    return lax.dot_general(a, b, (((1,), (1,)), ((), ())), preferred_element_type=F32)


def one_hot(mask):
    return jnp.where(mask, 1.0, 0.0)


def tables(ids, probs, left_ref, combine_ref, spare_ref):
    expert = iota((EXPERTS, TOK), 0)
    member = jnp.zeros((EXPERTS, TOK), F32)
    weight = jnp.zeros((EXPERTS, TOK), F32)
    for k in range(TOP):
        hit = ids[k : k + 1, :] == expert
        member = member + jnp.where(hit, 1.0, 0.0)
        weight = weight + jnp.where(hit, probs[k : k + 1, :], 0.0)
    member = member.astype(BF16)
    before = one_hot(iota((TOK, TOK), 0) < iota((TOK, TOK), 1)).astype(BF16)
    rank = product(member, before).astype(BF16)
    widen = one_hot(iota((ROWS8, EXPERTS), 0) // PACKED == iota((ROWS8, EXPERTS), 1)).astype(BF16)
    member8 = product(widen, member)
    rank8 = jnp.where(member8 > 0.5, product(widen, rank), -1.0)
    weight8 = product(widen, weight.astype(BF16))
    place = iota((ROWS8, TOK), 0) % PACKED
    own = one_hot((rank8 == place.astype(F32)) & (place < CAP))
    combine_ref[0] = own.T.astype(BF16)
    for g in range(3):
        goal = (place - CAP) * 3 + g
        tail = one_hot((rank8 == goal.astype(F32)) & (place >= CAP))
        combine_ref[g + 1] = tail.T.astype(BF16)
        left_ref[g] = jnp.concatenate([own, tail], axis=1).astype(BF16)
    prob = jnp.sum(own * weight8, axis=1, keepdims=True)
    row = iota((ROWS8, 128), 0)
    diagonal = jnp.where(row % PACKED == iota((ROWS8, 128), 1), prob, 0.0).astype(BF16)
    r = iota((ROWS8, ROWS8), 0)
    c = iota((ROWS8, ROWS8), 1)
    lift = one_hot((r // PACKED == c // PACKED) & (r % PACKED == CAP)).astype(BF16)
    spare_ref[...] = product(lift, diagonal).astype(BF16)


def spread(left_ref, x_ref, out_ref):
    rest = x_ref[:, WIDE:]
    for g in range(3):
        cols = pl.ds(g * TAIL, TAIL)
        right = jnp.concatenate([x_ref[:, cols], rest], axis=0)
        out_ref[:, cols] = product(left_ref[g], right).astype(BF16)
    return product(left_ref[0][:, :TOK], x_ref[:, 3 * TAIL : WIDE])


def spread_x_kernel(ids_ref, probs_ref, x_ref, out_ref, left_ref, combine_ref, spare_ref):
    @pl.when(pl.program_id(0) == 0)
    def _():
        tables(ids_ref[...], probs_ref[...], left_ref, combine_ref, spare_ref)

    out_ref[:, 3 * TAIL :] = spread(left_ref, x_ref, out_ref).astype(BF16)


def spread_dy_kernel(left_ref, spare_ref, x_ref, out_ref):
    last = spread(left_ref, x_ref, out_ref)
    out_ref[:, 3 * TAIL :] = last.astype(BF16) + spare_ref[...]


def unpack_masks(main_ref, tail_ref):
    r = iota((SLOTS, ROWS8), 0)
    c = iota((SLOTS, ROWS8), 1)
    same = r // CAP == c // PACKED
    slot = r % CAP
    place = c % PACKED
    main_ref[...] = one_hot(same & (slot == place)).astype(BF16)
    for g in range(3):
        tail = one_hot(same & (place >= CAP) & (slot == (place - CAP) * 3 + g))
        tail_ref[:, g * ROWS8 : (g + 1) * ROWS8] = tail.astype(BF16)


def stacked(packed):
    return jnp.concatenate([packed[:, g * TAIL : (g + 1) * TAIL] for g in range(3)], axis=0)


def unpack(main_ref, tail_ref, packed, rows_ref):
    rows_ref[:, :WIDE] = product(main_ref[...], packed).astype(BF16)
    rows_ref[:, WIDE:] = product(tail_ref[...], stacked(packed)).astype(BF16)


def unpack_all(packed_ref, rows_ref, main_ref, tail_ref):
    for j in range(packed_ref.shape[0] // ROWS8):
        rows = rows_ref.at[pl.ds(j * SLOTS, SLOTS)]
        unpack(main_ref, tail_ref, packed_ref[pl.ds(j * ROWS8, ROWS8), :], rows)


def shares(source, held, sems):
    count = sems.shape[0]
    rows = held.shape[0] // count
    parts = [pl.ds(i * rows, rows) for i in range(count)]
    return [
        pltpu.make_async_copy(source.at[part], held.at[part], sems.at[i])
        for i, part in enumerate(parts)
    ]


def start(copies):
    for copy in copies:
        copy.start()


def finish(copies):
    for copy in copies:
        copy.wait()


def ring_place(n):
    return jnp.bitwise_and(lax.axis_index("sp").astype(jnp.int32) + n, RING - 1)


def span(at, rows):
    return pl.ds(pl.multiple_of(at * rows, rows), rows)


def gate_up_kernel(
    packed_hbm,
    gate_hbm,
    up_hbm,
    rows_ref,
    parts_ref,
    packed_ref,
    packed_sem,
    gate_ref,
    up_ref,
    gate_sem,
    up_sem,
    *masks,
):
    step = pl.program_id(0)
    weights = ((gate_hbm, gate_ref, gate_sem), (up_hbm, up_ref, up_sem))
    rows8 = packed_ref.shape[0] // 2
    pieces = [
        pltpu.make_async_copy(
            packed_hbm.at[pl.ds(j * rows8, rows8)],
            packed_ref.at[pl.ds(j * rows8, rows8)],
            packed_sem.at[j],
        )
        for j in range(2)
    ]

    @pl.when(step == 0)
    def _():
        pieces[0].start()
        for weight in weights:
            start(shares(*weight))
        pieces[1].start()
        unpack_masks(*masks)

    for j in range(2):

        @pl.when(step == j)
        def _(j=j):
            pieces[j].wait()

    unpack_all(packed_ref.at[span(step, rows8)], rows_ref, *masks)
    hidden = gate_ref.shape[1]
    for j, weight in enumerate(weights):

        @pl.when(step == 0)
        def _(weight=weight):
            finish(shares(*weight))

        cols = pl.ds(j * hidden, hidden)
        parts_ref[:, cols] = product(rows_ref[...], weight[1][...]).astype(BF16)


def back_parts(rows_ref, down_ref, copies, outs):
    width = down_ref.shape[0] // len(copies)
    for j, copy in enumerate(copies):
        copy.wait()
        cols = pl.ds(j * width, width)
        part = product_t(rows_ref[...], down_ref[cols, :]).astype(BF16)
        for row, out_ref in outs:
            out_ref[:, cols] = part[row : row + out_ref.shape[0]]


def back_block_kernel(turns, packed_hbm, down_hbm, *refs):
    outs, rest = refs[:2], refs[2:]
    packed_ref, packed_sem, rows_ref, down_ref, sem, *masks = rest
    pieces = [
        pltpu.make_async_copy(
            packed_hbm.at[span(ring_place(n), ROWS8)],
            packed_ref.at[pl.ds(j * ROWS8, ROWS8)],
            packed_sem.at[j],
        )
        for j, n in enumerate(turns)
    ]
    copies = shares(down_hbm, down_ref, sem)
    start(pieces)
    start(copies)
    unpack_masks(*masks)
    finish(pieces)
    unpack_all(packed_ref, rows_ref, *masks)
    back_parts(rows_ref, down_ref, copies, ((0, outs[0]), (outs[0].shape[0], outs[1])))


def back_own_kernel(packed_ref, down_hbm, rows_ref, own_ref, prob_ref, down_ref, sem, *masks):
    copies = shares(down_hbm, down_ref, sem)
    start(copies)
    unpack_masks(*masks)
    unpack_all(packed_ref, rows_ref, *masks)
    own = ring_place(0)
    back_parts(rows_ref.at[span(own, SLOTS)], down_ref, copies, ((0, own_ref),))
    r = iota((SLOTS, ROWS8), 0)
    c = iota((SLOTS, ROWS8), 1)
    pick = one_hot((r // CAP == c // PACKED) & (c % PACKED == CAP)).astype(BF16)
    mine = iota((SLOTS, 128), 0) % CAP == iota((SLOTS, 128), 1)
    probs = product(pick, packed_ref[span(own, ROWS8), 3 * TAIL :])
    prob = jnp.sum(jnp.where(mine, probs, 0.0), axis=1, keepdims=True)
    prob_ref[...] = jnp.broadcast_to(prob, (SLOTS, 128)).astype(BF16)


def join_kernel(below_ref, above_ref, first_ref, second_ref, below_out, above_out):
    half = first_ref.shape[0]
    below_out[:half] = below_ref[:half]
    below_out[half:] = (below_ref[half:].astype(F32) + second_ref[...].astype(F32)).astype(BF16)
    above_out[:half] = (above_ref[:half].astype(F32) + first_ref[...].astype(F32)).astype(BF16)
    above_out[half:] = above_ref[half:]


def activate_kernel(
    gate_up_ref, own_ref, left_ref, right_ref, prob_ref, first_ref, second_ref, weighted_ref, slot_ref
):
    rows, hidden = own_ref.shape
    half = first_ref.shape[0]
    step = 32
    for start in range(0, rows, step):
        at = pl.ds(start, step)
        grads_ref = first_ref if start < half else second_ref
        to = pl.ds(start % half, step)
        gate = gate_up_ref[at, :hidden].astype(F32)
        up = gate_up_ref[at, hidden:].astype(F32)
        back = own_ref[at, :].astype(F32) + left_ref[at, :].astype(F32)
        back = back + right_ref[at, :].astype(F32)
        weight = prob_ref[at, :1].astype(F32)
        sigmoid = 1.0 / (1.0 + jnp.exp(-gate))
        swish = gate * sigmoid
        act = swish * up
        grad_act = weight * back
        grad_gate = grad_act * up * sigmoid * (1.0 + gate * (1.0 - sigmoid))
        grads_ref[to, :hidden] = grad_gate.astype(BF16)
        grads_ref[to, hidden:] = (grad_act * swish).astype(BF16)
        weighted_ref[at, :] = (weight * act).astype(BF16)
        slot = jnp.sum(back * act, axis=1, keepdims=True)
        mine = (start + iota((step, 128), 0)) % CAP == iota((step, 128), 1)
        slot_ref[at, :] = jnp.where(mine, slot, 0.0).astype(BF16)


def pack_group(g, rows_ref, out_ref, spare=None):
    r = iota((ROWS8, SLOTS), 0)
    c = iota((ROWS8, SLOTS), 1)
    same = r // PACKED == c // CAP
    place = r % PACKED
    slot = c % CAP
    main = one_hot(same & (slot == place)).astype(BF16)
    if g < 3:
        cols = pl.ds(g * TAIL, TAIL)
        tail = one_hot(same & (place >= CAP) & (slot == (place - CAP) * 3 + g)).astype(BF16)
        left = jnp.concatenate([main, tail], axis=1)
        right = jnp.concatenate([rows_ref[:, cols], rows_ref[:, WIDE:]], axis=0)
        out_ref[:, cols] = product(left, right).astype(BF16)
        return
    last = product(main, rows_ref[:, 3 * TAIL : WIDE])
    if spare is not None:
        lift = one_hot(same & (place == CAP)).astype(BF16)
        last = last + product(lift, spare)
    out_ref[:, 3 * TAIL :] = last.astype(BF16)


COLUMN_RUNS = ((WIDE, QUARTER, ()), (0, 2 * TAIL, (0, 1)), (2 * TAIL, WIDE, (2, 3)))


def row_grad_kernel(turns, own, *refs):
    halves = 2 * len(turns)
    halves_hbm, rest = refs[:halves], refs[halves:]
    gate_hbm, up_hbm, extra_ref, out_hbm, grads_ref, rows_ref, packed_ref, gate_ref, up_ref = rest[:9]
    grads_sem, gate_sem, up_sem, out_sem = rest[9:]
    hidden = gate_ref.shape[1]
    half = SLOTS // 2
    grads = [
        pltpu.make_async_copy(h, grads_ref.at[pl.ds(i * half, half)], grads_sem.at[i])
        for i, h in enumerate(halves_hbm)
    ]
    start(grads)
    pairs = []
    for i, (low, high, _) in enumerate(COLUMN_RUNS):
        run = pl.ds(low, high - low)
        pair = (
            pltpu.make_async_copy(gate_hbm.at[run], gate_ref.at[run], gate_sem.at[i]),
            pltpu.make_async_copy(up_hbm.at[run], up_ref.at[run], up_sem.at[i]),
        )
        start(pair)
        pairs.append(pair)
    finish(grads)
    spare = extra_ref[...] if own else None
    sent = []
    for (low, high, groups), pair in zip(COLUMN_RUNS, pairs):
        finish(pair)
        run = pl.ds(low, high - low)
        rows = product_t(grads_ref[:, :hidden], gate_ref[run, :])
        rows = rows + product_t(grads_ref[:, hidden:], up_ref[run, :])
        rows_ref[:, run] = rows.astype(BF16)
        for j, n in enumerate(turns):
            there = packed_ref.at[pl.ds(j * ROWS8, ROWS8)]
            for g in groups:
                pack_group(g, rows_ref.at[pl.ds(j * SLOTS, SLOTS)], there, spare)
            if groups:
                copy = pltpu.make_async_copy(
                    there.at[:, run],
                    out_hbm.at[span(ring_place(n), ROWS8), run],
                    out_sem.at[len(sent)],
                )
                copy.start()
                sent.append(copy)
    finish(sent)


def assemble_kernel(*refs):
    halves_hbm, out_ref, sem = refs[:8], refs[8], refs[9]
    half = SLOTS // 2
    copies = []
    for i, h in enumerate(halves_hbm):
        row = pl.multiple_of(ring_place((0, RING - 1, 1, 2)[i // 2]) * SLOTS + i % 2 * half, half)
        copies.append(pltpu.make_async_copy(h, out_ref.at[pl.ds(row, half)], sem.at[i]))
    start(copies)
    finish(copies)


def combine_kernel(ids_ref, left_ref, combine_ref, packed_ref, out_ref, probs_ref, slot_ref):
    step = pl.program_id(0)
    packed = packed_ref[...]
    out_ref[:, :WIDE] = product(combine_ref[0], packed).astype(BF16)
    tails = jnp.concatenate([combine_ref[g + 1] for g in range(3)], axis=1)
    out_ref[:, WIDE:] = product(tails, stacked(packed)).astype(BF16)
    spare = packed[:, 3 * TAIL :].astype(F32)

    @pl.when(step == 0)
    def _():
        slot_ref[...] = spare

    @pl.when(step > 0)
    def _():
        slot_ref[...] += spare

    @pl.when(step == pl.num_programs(0) - 1)
    def _():
        row = iota((ROWS8, 128), 0)
        slots = jnp.where(row % PACKED == CAP, slot_ref[...], 0.0).astype(BF16)
        r = iota((ROWS8, ROWS8), 0)
        c = iota((ROWS8, ROWS8), 1)
        group = one_hot(r // PACKED == c // PACKED).astype(BF16)
        wide = product(group, slots)
        mine = iota((ROWS8, 128), 1) == row % PACKED
        column = jnp.sum(jnp.where(mine, wide, 0.0), axis=1, keepdims=True)
        value = (left_ref[0, :, :TOK].astype(F32) * column).astype(BF16)
        gather = one_hot(iota((EXPERTS, ROWS8), 1) // PACKED == iota((EXPERTS, ROWS8), 0))
        table = product(gather.astype(BF16), value)
        expert = iota((EXPERTS, TOK), 0)
        found = [
            jnp.sum(jnp.where(ids_ref[k : k + 1, :] == expert, table, 0.0), axis=0, keepdims=True)
            for k in range(TOP)
        ]
        probs_ref[...] = jnp.concatenate(found, axis=0).astype(BF16)


def call(kernel, grid, ins, outs, scratch=(), flops=0, moved=0, aliases=None):
    return pl.pallas_call(
        kernel,
        grid_spec=pltpu.PrefetchScalarGridSpec(
            num_scalar_prefetch=0,
            grid=(grid,),
            in_specs=ins,
            out_specs=[s for s, _, _ in outs],
            scratch_shapes=list(scratch),
        ),
        out_shape=[place(shape, kind) for _, (shape, kind), place in outs],
        compiler_params=pltpu.CompilerParams(
            dimension_semantics=("arbitrary",), vmem_limit_bytes=24 * MIB
        ),
        input_output_aliases=aliases or {},
        cost_estimate=pl.CostEstimate(flops=flops, bytes_accessed=moved, transcendentals=0),
    )


def whole(*shape):
    return pl.BlockSpec(shape, lambda *i: (0,) * len(shape))


def rows_of(rows, cols):
    return pl.BlockSpec((rows, cols), lambda i, *_: (i, 0))


def cols_of(rows, cols):
    return pl.BlockSpec((rows, cols), lambda i, *_: (0, i))


ANY = pl.BlockSpec(memory_space=pl.ANY)


def on_device(hidden_in, grad_out, route_ids, route_probs, w_gate, w_up, w_down):
    sp_count = lax.axis_size("sp")
    pieces = lax.axis_size("ep") * sp_count
    hidden = w_gate.shape[2]
    model = hidden_in.shape[1]
    all_rows = pieces * CAP
    packed8 = pieces * PACKED
    gate_weight, up_weight, down_weight = w_gate[0], w_up[0], w_down[0]
    ids, probs = route_ids.T, route_probs.T

    def in_hbm(array):
        return pltpu.with_memory_space_constraint(array, pltpu.HBM)

    hidden_in, grad_out = in_hbm(hidden_in), in_hbm(grad_out)
    far, near = pltpu.HBM, jax.ShapeDtypeStruct
    tie = lax.optimization_barrier
    packet = (rows_of(ROWS8, WIDE), ((packed8, WIDE), BF16), far)
    x_send, left, combine, spare = call(
        spread_x_kernel,
        sp_count,
        [whole(TOP, TOK), whole(TOP, TOK), cols_of(TOK, QUARTER)],
        [
            packet,
            (whole(3, ROWS8, ROWS8), ((3, ROWS8, ROWS8), BF16), far),
            (whole(4, TOK, ROWS8), ((4, TOK, ROWS8), BF16), far),
            (whole(ROWS8, 128), ((ROWS8, 128), BF16), far),
        ],
        flops=2 * packed8 * WIDE * 256,
        moved=2 * (packed8 * WIDE + TOK * model),
    )(in_hbm(ids), in_hbm(probs), hidden_in)
    (dy_send,) = call(
        spread_dy_kernel,
        sp_count,
        [whole(3, ROWS8, ROWS8), whole(ROWS8, 128), cols_of(TOK, QUARTER)],
        [packet],
        flops=2 * packed8 * WIDE * 256,
        moved=2 * (packed8 * WIDE + TOK * model),
    )(in_hbm(left), in_hbm(spare), grad_out)

    def exchange(packed):
        pieced = packed.reshape(pieces, PACKED, WIDE)
        moved = lax.all_to_all(pieced, ("sp", "ep"), split_axis=0, concat_axis=0, tiled=True)
        return moved.reshape(packed8, WIDE)

    gate_weight, up_weight, down_weight = map(in_hbm, (gate_weight, up_weight, down_weight))
    x_packed = exchange(x_send)
    x_packed, dy_send = tie((in_hbm(x_packed), dy_send))
    dy_packed = exchange(dy_send)
    masks = (pltpu.VMEM((SLOTS, ROWS8), BF16), pltpu.VMEM((SLOTS, 3 * ROWS8), BF16))
    two_weights = (pltpu.VMEM((QUARTER, hidden), BF16),) * 2 + (pltpu.SemaphoreType.DMA((4,)),) * 2
    down_space = (pltpu.VMEM((hidden, QUARTER), BF16), pltpu.SemaphoreType.DMA((4,)))
    some_rows = all_rows // 2
    x_rows, gate_up_part = call(
        gate_up_kernel,
        2,
        [ANY, ANY, ANY],
        [
            (rows_of(some_rows, QUARTER), ((all_rows, QUARTER), BF16), far),
            (rows_of(some_rows, 2 * hidden), ((all_rows, 2 * hidden), BF16), far),
        ],
        (pltpu.VMEM((packed8, WIDE), BF16), pltpu.SemaphoreType.DMA((2,)), *two_weights, *masks),
        flops=4 * all_rows * QUARTER * hidden,
        moved=2 * (packed8 * WIDE + 2 * QUARTER * hidden + all_rows * (QUARTER + 2 * hidden)),
    )(x_packed, gate_weight, up_weight)
    gate_up = lax.psum_scatter(gate_up_part, "sp", scatter_dimension=0, tiled=True)
    own_rows = all_rows // sp_count
    half = own_rows // 2
    upward = [(i, (i + 1) % sp_count) for i in range(sp_count)]
    downward = [(i, (i - 1) % sp_count) for i in range(sp_count)]

    def both_ways(up, down):
        return lax.ppermute(up, "sp", upward), lax.ppermute(down, "sp", downward)

    dy_packed, _ = tie((dy_packed, gate_up_part))
    piece = ((half, hidden), BF16)
    block = ((own_rows, hidden), BF16)

    def back_space(turns):
        return (
            pltpu.VMEM((turns * ROWS8, WIDE), BF16),
            pltpu.SemaphoreType.DMA((turns,)),
            pltpu.VMEM((turns * SLOTS, QUARTER), BF16),
            *down_space,
            *masks,
        )

    far_first, far_second = call(
        functools.partial(back_block_kernel, (2,)),
        1,
        [ANY, ANY],
        [(whole(*piece[0]), piece, near)] * 2,
        back_space(1),
        flops=32 * 2 * all_rows * QUARTER * hidden,
        moved=2 * (packed8 * WIDE + QUARTER * hidden + all_rows * QUARTER),
    )(dy_packed, down_weight)
    far_first, far_second = both_ways(far_first, far_second)
    back_below, back_above = call(
        functools.partial(back_block_kernel, (sp_count - 1, 1)),
        1,
        [ANY, ANY],
        [(whole(*block[0]), block, near)] * 2,
        back_space(2),
        flops=2 * 2 * own_rows * QUARTER * hidden,
        moved=2 * (QUARTER * hidden + 2 * ROWS8 * WIDE + 2 * own_rows * hidden),
    )(dy_packed, down_weight)
    back_below, back_above = call(
        join_kernel,
        1,
        [whole(*block[0])] * 2 + [whole(*piece[0])] * 2,
        [(whole(*block[0]), block, near)] * 2,
        moved=2 * 5 * own_rows * hidden,
    )(back_below, back_above, far_first, far_second)
    left_part, right_part = both_ways(back_above, back_below)
    dy_late, _ = tie((dy_packed, back_above))
    dy_rows, back_own, prob_own = call(
        back_own_kernel,
        1,
        [whole(packed8, WIDE), ANY],
        [
            (whole(all_rows, QUARTER), ((all_rows, QUARTER), BF16), far),
            (whole(*block[0]), block, far),
            (whole(own_rows, 128), ((own_rows, 128), BF16), far),
        ],
        (*down_space, *masks),
        flops=2 * own_rows * QUARTER * hidden,
        moved=2 * (QUARTER * hidden + packed8 * WIDE + all_rows * QUARTER + own_rows * hidden),
    )(dy_late, down_weight)
    first, second, weighted_own, slot_own = call(
        activate_kernel,
        1,
        [whole(own_rows, 2 * hidden)] + [whole(*block[0])] * 3 + [whole(own_rows, 128)],
        [
            (whole(half, 2 * hidden), ((half, 2 * hidden), BF16), far),
            (whole(half, 2 * hidden), ((half, 2 * hidden), BF16), far),
            (whole(own_rows, hidden), ((own_rows, hidden), BF16), far),
            (whole(own_rows, 128), ((own_rows, 128), BF16), far),
        ],
        flops=20 * own_rows * hidden,
        moved=12 * own_rows * hidden,
    )(in_hbm(gate_up), in_hbm(back_own), left_part, right_part, in_hbm(prob_own))
    below_first, above_second = both_ways(first, second)
    below_second, above_first = both_ways(second, first)

    def row_grad(turns, grads, extra, own_block=False):
        count = len(grads)
        blocks = len(turns)
        dma = pltpu.SemaphoreType.DMA
        return call(
            functools.partial(row_grad_kernel, turns, own_block),
            1,
            [ANY] * (count + 2) + [whole(own_rows, 128) if own_block else ANY],
            [(ANY, ((packed8, WIDE), BF16), far)],
            (
                pltpu.VMEM((blocks * SLOTS, 2 * hidden), BF16),
                pltpu.VMEM((blocks * SLOTS, QUARTER), BF16),
                pltpu.VMEM((blocks * ROWS8, WIDE), BF16),
                pltpu.VMEM((QUARTER, hidden), BF16),
                pltpu.VMEM((QUARTER, hidden), BF16),
                dma((count,)),
                dma((3,)),
                dma((3,)),
                dma((2 * blocks,)),
            ),
            aliases={} if own_block else {count + 2: 0},
            flops=4 * blocks * own_rows * QUARTER * hidden,
            moved=2 * (2 * QUARTER * hidden + blocks * (ROWS8 * WIDE + own_rows * 2 * hidden)),
        )(*grads, gate_weight, up_weight, extra)[0]

    own_halves = (in_hbm(first), in_hbm(second))
    back_send = row_grad((0,), own_halves, in_hbm(slot_own), own_block=True)
    below_first, above_second, back_send = tie((below_first, above_second, back_send))
    across_first, across_second = both_ways(below_first, above_second)
    near_halves = (below_first, below_second, above_first, above_second)
    back_send = row_grad((sp_count - 1, 1), near_halves, back_send)
    across_first, across_second, back_send = tie((across_first, across_second, back_send))
    weighted_own, _, _ = tie((weighted_own, below_second, above_first))
    weighted = lax.all_gather(weighted_own, "sp", axis=0, tiled=True)
    back_send = row_grad((2,), (across_first, across_second), back_send)
    back_packed = exchange(back_send)
    (grads_all,) = call(
        assemble_kernel,
        1,
        [ANY] * 8,
        [(whole(all_rows, 2 * hidden), ((all_rows, 2 * hidden), BF16), near)],
        (pltpu.SemaphoreType.DMA((8,)),),
        moved=2 * 2 * all_rows * 2 * hidden,
    )(*tie((*own_halves, *near_halves, across_first, across_second, back_send))[:8])
    contract_rows = (((0,), (0,)), ((), ()))

    def over_rows(a, b):
        return lax.dot_general(a, b, contract_rows, preferred_element_type=F32).astype(BF16)

    grad_gate_weight = over_rows(x_rows, grads_all[:, :hidden])
    grad_up_weight = over_rows(x_rows, grads_all[:, hidden:])
    grad_down_weight = over_rows(weighted, dy_rows)
    grad_in, grad_probs = call(
        combine_kernel,
        sp_count,
        [whole(TOP, TOK), whole(3, ROWS8, ROWS8), whole(4, TOK, ROWS8), rows_of(ROWS8, WIDE)],
        [
            (cols_of(TOK, QUARTER), ((TOK, model), BF16), near),
            (whole(TOP, TOK), ((TOP, TOK), BF16), near),
        ],
        (pltpu.VMEM((ROWS8, 128), F32),),
        flops=2 * packed8 * WIDE * TOK * 2,
        moved=2 * (packed8 * WIDE + TOK * model),
    )(ids, left, combine, back_packed)
    return (
        grad_in,
        grad_gate_weight[None],
        grad_up_weight[None],
        grad_down_weight[None],
        grad_probs.T,
    )


def solution(mesh):
    placed = (
        P(("ep", "sp"), None),
        P(("ep", "sp"), None),
        P(("ep", "sp"), None),
        P(("ep", "sp"), None),
        P("ep", "sp", None),
        P("ep", "sp", None),
        P("ep", None, "sp"),
    )
    return jax.shard_map(
        on_device,
        mesh=mesh,
        in_specs=placed,
        out_specs=(
            P(("ep", "sp"), None),
            P("ep", "sp", None),
            P("ep", "sp", None),
            P("ep", None, "sp"),
            P(("ep", "sp"), None),
        ),
        check_vma=False,
    )
```

```python
import functools

import jax
import jax.numpy as jnp
from jax import lax
from jax.experimental import pallas as pl
from jax.experimental.pallas import tpu as pltpu
from jax.sharding import PartitionSpec as P

CAP = 6
EXPERTS = 32
TOK = 128
TOP = 8
WIDE = 1280
TAIL = 384
QUARTER = WIDE + TAIL
PACKED = 8
BLOCK = 32
SLOTS = BLOCK * CAP
ROWS8 = BLOCK * PACKED
RING = 4
MIB = 1 << 20
BF16 = jnp.bfloat16
F32 = jnp.float32


def iota(shape, dim):
    return lax.broadcasted_iota(jnp.int32, shape, dim)


def product(a, b):
    return jnp.dot(a, b, preferred_element_type=F32)


def product_t(a, b):
    return lax.dot_general(a, b, (((1,), (1,)), ((), ())), preferred_element_type=F32)


def one_hot(mask):
    return jnp.where(mask, 1.0, 0.0)


def ranked(ids, probs=None):
    expert = iota((EXPERTS, TOK), 0)
    member = jnp.zeros((EXPERTS, TOK), F32)
    weight = jnp.zeros((EXPERTS, TOK), F32)
    for k in range(TOP):
        hit = ids[k : k + 1, :] == expert
        member = member + jnp.where(hit, 1.0, 0.0)
        if probs is not None:
            weight = weight + jnp.where(hit, probs[k : k + 1, :], 0.0)
    member = member.astype(BF16)
    before = one_hot(iota((TOK, TOK), 0) < iota((TOK, TOK), 1)).astype(BF16)
    rank = jnp.where(member > 0.5, product(member, before), -1.0).astype(BF16)
    widen = one_hot(iota((ROWS8, EXPERTS), 0) // PACKED == iota((ROWS8, EXPERTS), 1)).astype(BF16)
    rank8 = product(widen, rank)
    weight8 = None if probs is None else product(widen, weight.astype(BF16))
    return iota((ROWS8, TOK), 0) % PACKED, rank8, weight8


def tables(ids, left_ref):
    place, rank8, _ = ranked(ids)
    own = one_hot((rank8 == place.astype(F32)) & (place < CAP))
    for g in range(3):
        goal = (place - CAP) * 3 + g
        tail = one_hot((rank8 == goal.astype(F32)) & (place >= CAP))
        left_ref[g] = jnp.concatenate([own, tail], axis=1).astype(BF16)


def late_tables(ids, probs, left_ref, combine_ref, spare_ref):
    _, _, weight8 = ranked(ids, probs)
    own = left_ref[0, :, :TOK].astype(F32)
    combine_ref[0] = own.T.astype(BF16)
    for g in range(3):
        combine_ref[g + 1] = left_ref[g, :, TOK:].astype(F32).T.astype(BF16)
    prob = jnp.sum(own * weight8, axis=1, keepdims=True)
    row = iota((ROWS8, 128), 0)
    diagonal = jnp.where(row % PACKED == iota((ROWS8, 128), 1), prob, 0.0).astype(BF16)
    r = iota((ROWS8, ROWS8), 0)
    c = iota((ROWS8, ROWS8), 1)
    lift = one_hot((r // PACKED == c // PACKED) & (r % PACKED == CAP)).astype(BF16)
    spare_ref[...] = product(lift, diagonal).astype(BF16)


def spread(left_ref, x_ref, out_ref):
    rest = x_ref[:, WIDE:]
    for g in range(3):
        cols = pl.ds(g * TAIL, TAIL)
        right = jnp.concatenate([x_ref[:, cols], rest], axis=0)
        out_ref[:, cols] = product(left_ref[g], right).astype(BF16)
    return product(left_ref[0][:, :TOK], x_ref[:, 3 * TAIL : WIDE])


def spread_x_kernel(ids_ref, x_ref, out_ref, left_ref):
    @pl.when(pl.program_id(0) == 0)
    def _():
        tables(ids_ref[...], left_ref)

    out_ref[:, 3 * TAIL :] = spread(left_ref, x_ref, out_ref).astype(BF16)


def spread_dy_kernel(ids_ref, probs_ref, left_ref, x_ref, out_ref, combine_ref, spare_ref):
    @pl.when(pl.program_id(0) == 0)
    def _():
        late_tables(ids_ref[...], probs_ref[...], left_ref, combine_ref, spare_ref)

    last = spread(left_ref, x_ref, out_ref)
    out_ref[:, 3 * TAIL :] = last.astype(BF16) + spare_ref[...]


def unpack_masks(main_ref, tail_ref):
    r = iota((SLOTS, ROWS8), 0)
    c = iota((SLOTS, ROWS8), 1)
    same = r // CAP == c // PACKED
    slot = r % CAP
    place = c % PACKED
    main_ref[...] = one_hot(same & (slot == place)).astype(BF16)
    for g in range(3):
        tail = one_hot(same & (place >= CAP) & (slot == (place - CAP) * 3 + g))
        tail_ref[:, g * ROWS8 : (g + 1) * ROWS8] = tail.astype(BF16)


def stacked(packed):
    return jnp.concatenate([packed[:, g * TAIL : (g + 1) * TAIL] for g in range(3)], axis=0)


def unpack(main_ref, tail_ref, packed, rows_ref):
    rows_ref[:, :WIDE] = product(main_ref[...], packed).astype(BF16)
    rows_ref[:, WIDE:] = product(tail_ref[...], stacked(packed)).astype(BF16)


def unpack_all(packed_ref, rows_ref, main_ref, tail_ref):
    for j in range(packed_ref.shape[0] // ROWS8):
        rows = rows_ref.at[pl.ds(j * SLOTS, SLOTS)]
        unpack(main_ref, tail_ref, packed_ref[pl.ds(j * ROWS8, ROWS8), :], rows)


def shares(source, held, sems):
    count = sems.shape[0]
    rows = held.shape[0] // count
    parts = [pl.ds(i * rows, rows) for i in range(count)]
    return [
        pltpu.make_async_copy(source.at[part], held.at[part], sems.at[i])
        for i, part in enumerate(parts)
    ]


def start(copies):
    for copy in copies:
        copy.start()


def finish(copies):
    for copy in copies:
        copy.wait()


def ring_place(n):
    return jnp.bitwise_and(lax.axis_index("sp").astype(jnp.int32) + n, RING - 1)


def span(at, rows):
    return pl.ds(pl.multiple_of(at * rows, rows), rows)


def gate_up_kernel(
    packed_hbm,
    gate_hbm,
    up_hbm,
    rows_ref,
    parts_ref,
    packed_ref,
    packed_sem,
    gate_ref,
    up_ref,
    gate_sem,
    up_sem,
    *masks,
):
    step = pl.program_id(0)
    weights = ((gate_hbm, gate_ref, gate_sem), (up_hbm, up_ref, up_sem))
    rows8 = packed_ref.shape[0] // 2
    pieces = [
        pltpu.make_async_copy(
            packed_hbm.at[pl.ds(j * rows8, rows8)],
            packed_ref.at[pl.ds(j * rows8, rows8)],
            packed_sem.at[j],
        )
        for j in range(2)
    ]

    @pl.when(step == 0)
    def _():
        pieces[0].start()
        for weight in weights:
            start(shares(*weight))
        pieces[1].start()
        unpack_masks(*masks)

    for j in range(2):

        @pl.when(step == j)
        def _(j=j):
            pieces[j].wait()

    unpack_all(packed_ref.at[span(step, rows8)], rows_ref, *masks)
    hidden = gate_ref.shape[1]
    for j, weight in enumerate(weights):

        @pl.when(step == 0)
        def _(weight=weight):
            finish(shares(*weight))

        cols = pl.ds(j * hidden, hidden)
        parts_ref[:, cols] = product(rows_ref[...], weight[1][...]).astype(BF16)


def back_parts(rows_ref, down_ref, copies, outs):
    width = down_ref.shape[0] // len(copies)
    for j, copy in enumerate(copies):
        copy.wait()
        cols = pl.ds(j * width, width)
        part = product_t(rows_ref[...], down_ref[cols, :]).astype(BF16)
        for row, out_ref in outs:
            out_ref[:, cols] = part[row : row + out_ref.shape[0]]


def back_block_kernel(turns, packed_hbm, down_hbm, *refs):
    outs, rest = refs[:2], refs[2:]
    packed_ref, packed_sem, rows_ref, down_ref, sem, *masks = rest
    pieces = [
        pltpu.make_async_copy(
            packed_hbm.at[span(ring_place(n), ROWS8)],
            packed_ref.at[pl.ds(j * ROWS8, ROWS8)],
            packed_sem.at[j],
        )
        for j, n in enumerate(turns)
    ]
    copies = shares(down_hbm, down_ref, sem)
    start(pieces)
    start(copies)
    unpack_masks(*masks)
    finish(pieces)
    unpack_all(packed_ref, rows_ref, *masks)
    back_parts(rows_ref, down_ref, copies, ((0, outs[0]), (outs[0].shape[0], outs[1])))


def back_own_kernel(packed_ref, down_hbm, rows_ref, own_ref, prob_ref, down_ref, sem, *masks):
    copies = shares(down_hbm, down_ref, sem)
    start(copies)
    unpack_masks(*masks)
    unpack_all(packed_ref, rows_ref, *masks)
    own = ring_place(0)
    back_parts(rows_ref.at[span(own, SLOTS)], down_ref, copies, ((0, own_ref),))
    r = iota((SLOTS, ROWS8), 0)
    c = iota((SLOTS, ROWS8), 1)
    pick = one_hot((r // CAP == c // PACKED) & (c % PACKED == CAP)).astype(BF16)
    mine = iota((SLOTS, 128), 0) % CAP == iota((SLOTS, 128), 1)
    probs = product(pick, packed_ref[span(own, ROWS8), 3 * TAIL :])
    prob = jnp.sum(jnp.where(mine, probs, 0.0), axis=1, keepdims=True)
    prob_ref[...] = jnp.broadcast_to(prob, (SLOTS, 128)).astype(BF16)


def join_kernel(below_ref, above_ref, first_ref, second_ref, below_out, above_out):
    half = first_ref.shape[0]
    below_out[:half] = below_ref[:half]
    below_out[half:] = (below_ref[half:].astype(F32) + second_ref[...].astype(F32)).astype(BF16)
    above_out[:half] = (above_ref[:half].astype(F32) + first_ref[...].astype(F32)).astype(BF16)
    above_out[half:] = above_ref[half:]


def activate_kernel(
    gate_up_ref, own_ref, left_ref, right_ref, prob_ref, first_ref, second_ref, weighted_ref, slot_ref
):
    rows, hidden = own_ref.shape
    half = first_ref.shape[0]
    step = 32
    for start in range(0, rows, step):
        at = pl.ds(start, step)
        grads_ref = first_ref if start < half else second_ref
        to = pl.ds(start % half, step)
        gate = gate_up_ref[at, :hidden].astype(F32)
        up = gate_up_ref[at, hidden:].astype(F32)
        back = own_ref[at, :].astype(F32) + left_ref[at, :].astype(F32)
        back = back + right_ref[at, :].astype(F32)
        weight = prob_ref[at, :1].astype(F32)
        sigmoid = 1.0 / (1.0 + jnp.exp(-gate))
        swish = gate * sigmoid
        act = swish * up
        grad_act = weight * back
        grad_gate = grad_act * up * sigmoid * (1.0 + gate * (1.0 - sigmoid))
        grads_ref[to, :hidden] = grad_gate.astype(BF16)
        grads_ref[to, hidden:] = (grad_act * swish).astype(BF16)
        weighted_ref[at, :] = (weight * act).astype(BF16)
        slot = jnp.sum(back * act, axis=1, keepdims=True)
        mine = (start + iota((step, 128), 0)) % CAP == iota((step, 128), 1)
        slot_ref[at, :] = jnp.where(mine, slot, 0.0).astype(BF16)


def pack_group(g, rows_ref, out_ref, spare=None):
    r = iota((ROWS8, SLOTS), 0)
    c = iota((ROWS8, SLOTS), 1)
    same = r // PACKED == c // CAP
    place = r % PACKED
    slot = c % CAP
    main = one_hot(same & (slot == place)).astype(BF16)
    if g < 3:
        cols = pl.ds(g * TAIL, TAIL)
        tail = one_hot(same & (place >= CAP) & (slot == (place - CAP) * 3 + g)).astype(BF16)
        left = jnp.concatenate([main, tail], axis=1)
        right = jnp.concatenate([rows_ref[:, cols], rows_ref[:, WIDE:]], axis=0)
        out_ref[:, cols] = product(left, right).astype(BF16)
        return
    last = product(main, rows_ref[:, 3 * TAIL : WIDE])
    if spare is not None:
        lift = one_hot(same & (place == CAP)).astype(BF16)
        last = last + product(lift, spare)
    out_ref[:, 3 * TAIL :] = last.astype(BF16)


COLUMN_RUNS = ((WIDE, QUARTER, ()), (0, 2 * TAIL, (0, 1)), (2 * TAIL, WIDE, (2, 3)))


def row_grad_kernel(turns, own, *refs):
    halves = 2 * len(turns)
    halves_hbm, rest = refs[:halves], refs[halves:]
    gate_hbm, up_hbm, extra_ref, out_hbm, grads_ref, rows_ref, packed_ref, gate_ref, up_ref = rest[:9]
    grads_sem, gate_sem, up_sem, out_sem = rest[9:]
    hidden = gate_ref.shape[1]
    half = SLOTS // 2
    grads = [
        pltpu.make_async_copy(h, grads_ref.at[pl.ds(i * half, half)], grads_sem.at[i])
        for i, h in enumerate(halves_hbm)
    ]
    start(grads)
    pairs = []
    for i, (low, high, _) in enumerate(COLUMN_RUNS):
        run = pl.ds(low, high - low)
        pair = (
            pltpu.make_async_copy(gate_hbm.at[run], gate_ref.at[run], gate_sem.at[i]),
            pltpu.make_async_copy(up_hbm.at[run], up_ref.at[run], up_sem.at[i]),
        )
        start(pair)
        pairs.append(pair)
    finish(grads)
    spare = extra_ref[...] if own else None
    sent = []
    for (low, high, groups), pair in zip(COLUMN_RUNS, pairs):
        finish(pair)
        run = pl.ds(low, high - low)
        rows = product_t(grads_ref[:, :hidden], gate_ref[run, :])
        rows = rows + product_t(grads_ref[:, hidden:], up_ref[run, :])
        rows_ref[:, run] = rows.astype(BF16)
        for j, n in enumerate(turns):
            there = packed_ref.at[pl.ds(j * ROWS8, ROWS8)]
            for g in groups:
                pack_group(g, rows_ref.at[pl.ds(j * SLOTS, SLOTS)], there, spare)
            if groups:
                copy = pltpu.make_async_copy(
                    there.at[:, run],
                    out_hbm.at[span(ring_place(n), ROWS8), run],
                    out_sem.at[len(sent)],
                )
                copy.start()
                sent.append(copy)
    finish(sent)


def assemble_kernel(*refs):
    halves_hbm, out_ref, sem = refs[:8], refs[8], refs[9]
    half = SLOTS // 2
    copies = []
    for i, h in enumerate(halves_hbm):
        row = pl.multiple_of(ring_place((0, RING - 1, 1, 2)[i // 2]) * SLOTS + i % 2 * half, half)
        copies.append(pltpu.make_async_copy(h, out_ref.at[pl.ds(row, half)], sem.at[i]))
    start(copies)
    finish(copies)


def combine_kernel(ids_ref, left_ref, combine_ref, packed_ref, out_hbm, probs_ref, out_ref, sem):
    tails = jnp.concatenate([combine_ref[g + 1] for g in range(3)], axis=1)
    spare = jnp.zeros((ROWS8, 128), F32)
    sent = []
    for q in range(packed_ref.shape[0] // ROWS8):
        rows = pl.ds(q * ROWS8, ROWS8)
        cols = pl.ds(q * QUARTER, QUARTER)
        low = q * QUARTER
        out_ref[:, low : low + WIDE] = product(combine_ref[0], packed_ref[rows, :]).astype(BF16)
        rest = product(tails, stacked(packed_ref[rows, :])).astype(BF16)
        out_ref[:, low + WIDE : low + QUARTER] = rest
        copy = pltpu.make_async_copy(out_ref.at[:, cols], out_hbm.at[:, cols], sem.at[q])
        copy.start()
        sent.append(copy)
        spare = spare + packed_ref[rows, 3 * TAIL :].astype(F32)
    row = iota((ROWS8, 128), 0)
    slots = jnp.where(row % PACKED == CAP, spare, 0.0).astype(BF16)
    r = iota((ROWS8, ROWS8), 0)
    c = iota((ROWS8, ROWS8), 1)
    group = one_hot(r // PACKED == c // PACKED).astype(BF16)
    wide = product(group, slots)
    mine = iota((ROWS8, 128), 1) == row % PACKED
    column = jnp.sum(jnp.where(mine, wide, 0.0), axis=1, keepdims=True)
    value = (left_ref[0, :, :TOK].astype(F32) * column).astype(BF16)
    gather = one_hot(iota((EXPERTS, ROWS8), 1) // PACKED == iota((EXPERTS, ROWS8), 0))
    table = product(gather.astype(BF16), value)
    expert = iota((EXPERTS, TOK), 0)
    found = [
        jnp.sum(jnp.where(ids_ref[k : k + 1, :] == expert, table, 0.0), axis=0, keepdims=True)
        for k in range(TOP)
    ]
    probs_ref[...] = jnp.concatenate(found, axis=0).astype(BF16)
    finish(sent)


def call(kernel, grid, ins, outs, scratch=(), flops=0, moved=0, aliases=None):
    return pl.pallas_call(
        kernel,
        grid_spec=pltpu.PrefetchScalarGridSpec(
            num_scalar_prefetch=0,
            grid=(grid,),
            in_specs=ins,
            out_specs=[s for s, _, _ in outs],
            scratch_shapes=list(scratch),
        ),
        out_shape=[place(shape, kind) for _, (shape, kind), place in outs],
        compiler_params=pltpu.CompilerParams(
            dimension_semantics=("arbitrary",), vmem_limit_bytes=24 * MIB
        ),
        input_output_aliases=aliases or {},
        cost_estimate=pl.CostEstimate(flops=flops, bytes_accessed=moved, transcendentals=0),
    )


def whole(*shape):
    return pl.BlockSpec(shape, lambda *i: (0,) * len(shape))


def rows_of(rows, cols):
    return pl.BlockSpec((rows, cols), lambda i, *_: (i, 0))


def cols_of(rows, cols):
    return pl.BlockSpec((rows, cols), lambda i, *_: (0, i))


ANY = pl.BlockSpec(memory_space=pl.ANY)
NEAR = pl.BlockSpec(memory_space=pltpu.VMEM)


def on_device(hidden_in, grad_out, route_ids, route_probs, w_gate, w_up, w_down):
    sp_count = lax.axis_size("sp")
    pieces = lax.axis_size("ep") * sp_count
    hidden = w_gate.shape[2]
    model = hidden_in.shape[1]
    all_rows = pieces * CAP
    packed8 = pieces * PACKED
    gate_weight, up_weight, down_weight = w_gate[0], w_up[0], w_down[0]
    ids, probs = route_ids.T, route_probs.T

    def in_hbm(array):
        return pltpu.with_memory_space_constraint(array, pltpu.HBM)

    hidden_in, grad_out = in_hbm(hidden_in), in_hbm(grad_out)
    far, near = pltpu.HBM, jax.ShapeDtypeStruct
    tie = lax.optimization_barrier
    packet = (rows_of(ROWS8, WIDE), ((packed8, WIDE), BF16), far)
    x_send, left = call(
        spread_x_kernel,
        sp_count,
        [whole(TOP, TOK), cols_of(TOK, QUARTER)],
        [packet, (whole(3, ROWS8, ROWS8), ((3, ROWS8, ROWS8), BF16), far)],
        flops=2 * packed8 * WIDE * 256,
        moved=2 * (packed8 * WIDE + TOK * model),
    )(in_hbm(ids), hidden_in)
    dy_send, combine = call(
        spread_dy_kernel,
        sp_count,
        [whole(TOP, TOK), whole(TOP, TOK), whole(3, ROWS8, ROWS8), cols_of(TOK, QUARTER)],
        [packet, (whole(4, TOK, ROWS8), ((4, TOK, ROWS8), BF16), far)],
        (pltpu.VMEM((ROWS8, 128), BF16),),
        flops=2 * packed8 * WIDE * 256,
        moved=2 * (packed8 * WIDE + TOK * model),
    )(in_hbm(ids), in_hbm(probs), in_hbm(left), grad_out)

    def exchange(packed):
        pieced = packed.reshape(pieces, PACKED, WIDE)
        moved = lax.all_to_all(pieced, ("sp", "ep"), split_axis=0, concat_axis=0, tiled=True)
        return moved.reshape(packed8, WIDE)

    gate_weight, up_weight, down_weight = map(in_hbm, (gate_weight, up_weight, down_weight))
    x_packed = exchange(x_send)
    x_packed, dy_send = tie((in_hbm(x_packed), dy_send))
    dy_packed = exchange(dy_send)
    masks = (pltpu.VMEM((SLOTS, ROWS8), BF16), pltpu.VMEM((SLOTS, 3 * ROWS8), BF16))
    two_weights = (pltpu.VMEM((QUARTER, hidden), BF16),) * 2 + (pltpu.SemaphoreType.DMA((4,)),) * 2
    down_space = (pltpu.VMEM((hidden, QUARTER), BF16), pltpu.SemaphoreType.DMA((4,)))
    some_rows = all_rows // 2
    x_rows, gate_up_part = call(
        gate_up_kernel,
        2,
        [ANY, ANY, ANY],
        [
            (rows_of(some_rows, QUARTER), ((all_rows, QUARTER), BF16), far),
            (rows_of(some_rows, 2 * hidden), ((all_rows, 2 * hidden), BF16), far),
        ],
        (pltpu.VMEM((packed8, WIDE), BF16), pltpu.SemaphoreType.DMA((2,)), *two_weights, *masks),
        flops=4 * all_rows * QUARTER * hidden,
        moved=2 * (packed8 * WIDE + 2 * QUARTER * hidden + all_rows * (QUARTER + 2 * hidden)),
    )(x_packed, gate_weight, up_weight)
    gate_up = lax.psum_scatter(gate_up_part, "sp", scatter_dimension=0, tiled=True)
    own_rows = all_rows // sp_count
    half = own_rows // 2
    upward = [(i, (i + 1) % sp_count) for i in range(sp_count)]
    downward = [(i, (i - 1) % sp_count) for i in range(sp_count)]

    def both_ways(up, down):
        return lax.ppermute(up, "sp", upward), lax.ppermute(down, "sp", downward)

    dy_packed, _ = tie((dy_packed, gate_up_part))
    piece = ((half, hidden), BF16)
    block = ((own_rows, hidden), BF16)

    def back_space(turns):
        return (
            pltpu.VMEM((turns * ROWS8, WIDE), BF16),
            pltpu.SemaphoreType.DMA((turns,)),
            pltpu.VMEM((turns * SLOTS, QUARTER), BF16),
            *down_space,
            *masks,
        )

    far_first, far_second = call(
        functools.partial(back_block_kernel, (2,)),
        1,
        [ANY, ANY],
        [(whole(*piece[0]), piece, near)] * 2,
        back_space(1),
        flops=32 * 2 * all_rows * QUARTER * hidden,
        moved=2 * (packed8 * WIDE + QUARTER * hidden + all_rows * QUARTER),
    )(dy_packed, down_weight)
    far_first, far_second = both_ways(far_first, far_second)
    back_below, back_above = call(
        functools.partial(back_block_kernel, (sp_count - 1, 1)),
        1,
        [ANY, ANY],
        [(whole(*block[0]), block, near)] * 2,
        back_space(2),
        flops=2 * 2 * own_rows * QUARTER * hidden,
        moved=2 * (QUARTER * hidden + 2 * ROWS8 * WIDE + 2 * own_rows * hidden),
    )(dy_packed, down_weight)
    back_below, back_above = call(
        join_kernel,
        1,
        [whole(*block[0])] * 2 + [whole(*piece[0])] * 2,
        [(whole(*block[0]), block, near)] * 2,
        moved=2 * 5 * own_rows * hidden,
    )(back_below, back_above, far_first, far_second)
    left_part, right_part = both_ways(back_above, back_below)
    dy_late, _ = tie((dy_packed, back_above))
    dy_rows, back_own, prob_own = call(
        back_own_kernel,
        1,
        [whole(packed8, WIDE), ANY],
        [
            (whole(all_rows, QUARTER), ((all_rows, QUARTER), BF16), far),
            (whole(*block[0]), block, far),
            (whole(own_rows, 128), ((own_rows, 128), BF16), far),
        ],
        (*down_space, *masks),
        flops=2 * own_rows * QUARTER * hidden,
        moved=2 * (QUARTER * hidden + packed8 * WIDE + all_rows * QUARTER + own_rows * hidden),
    )(dy_late, down_weight)
    first, second, weighted_own, slot_own = call(
        activate_kernel,
        1,
        [whole(own_rows, 2 * hidden)] + [whole(*block[0])] * 3 + [whole(own_rows, 128)],
        [
            (whole(half, 2 * hidden), ((half, 2 * hidden), BF16), far),
            (whole(half, 2 * hidden), ((half, 2 * hidden), BF16), far),
            (whole(own_rows, hidden), ((own_rows, hidden), BF16), far),
            (whole(own_rows, 128), ((own_rows, 128), BF16), far),
        ],
        flops=20 * own_rows * hidden,
        moved=12 * own_rows * hidden,
    )(in_hbm(gate_up), in_hbm(back_own), left_part, right_part, in_hbm(prob_own))
    below_first, above_second = both_ways(first, second)
    below_second, above_first = both_ways(second, first)

    def row_grad(turns, grads, extra, own_block=False):
        count = len(grads)
        blocks = len(turns)
        dma = pltpu.SemaphoreType.DMA
        return call(
            functools.partial(row_grad_kernel, turns, own_block),
            1,
            [ANY] * (count + 2) + [whole(own_rows, 128) if own_block else ANY],
            [(ANY, ((packed8, WIDE), BF16), far)],
            (
                pltpu.VMEM((blocks * SLOTS, 2 * hidden), BF16),
                pltpu.VMEM((blocks * SLOTS, QUARTER), BF16),
                pltpu.VMEM((blocks * ROWS8, WIDE), BF16),
                pltpu.VMEM((QUARTER, hidden), BF16),
                pltpu.VMEM((QUARTER, hidden), BF16),
                dma((count,)),
                dma((3,)),
                dma((3,)),
                dma((2 * blocks,)),
            ),
            aliases={} if own_block else {count + 2: 0},
            flops=4 * blocks * own_rows * QUARTER * hidden,
            moved=2 * (2 * QUARTER * hidden + blocks * (ROWS8 * WIDE + own_rows * 2 * hidden)),
        )(*grads, gate_weight, up_weight, extra)[0]

    own_halves = (in_hbm(first), in_hbm(second))
    back_send = row_grad((0,), own_halves, in_hbm(slot_own), own_block=True)
    below_first, above_second, back_send = tie((below_first, above_second, back_send))
    across_first, across_second = both_ways(below_first, above_second)
    near_halves = (below_first, below_second, above_first, above_second)
    back_send = row_grad((sp_count - 1, 1), near_halves, back_send)
    across_first, across_second, back_send = tie((across_first, across_second, back_send))
    weighted_own, _, _ = tie((weighted_own, below_second, above_first))
    weighted = lax.all_gather(weighted_own, "sp", axis=0, tiled=True)
    back_send = row_grad((2,), (across_first, across_second), back_send)
    back_packed = exchange(back_send)
    (grads_all,) = call(
        assemble_kernel,
        1,
        [ANY] * 8,
        [(whole(all_rows, 2 * hidden), ((all_rows, 2 * hidden), BF16), near)],
        (pltpu.SemaphoreType.DMA((8,)),),
        moved=2 * 2 * all_rows * 2 * hidden,
    )(*tie((*own_halves, *near_halves, across_first, across_second, back_send))[:8])
    contract_rows = (((0,), (0,)), ((), ()))

    def over_rows(a, b):
        return lax.dot_general(a, b, contract_rows, preferred_element_type=F32).astype(BF16)

    grad_gate_weight = over_rows(x_rows, grads_all[:, :hidden])
    grad_up_weight = over_rows(x_rows, grads_all[:, hidden:])
    grad_down_weight = over_rows(weighted, dy_rows)
    grad_in, grad_probs = call(
        combine_kernel,
        1,
        [NEAR, NEAR, NEAR, NEAR],
        [
            (ANY, ((TOK, model), BF16), far),
            (whole(TOP, TOK), ((TOP, TOK), BF16), near),
        ],
        (pltpu.VMEM((TOK, model), BF16), pltpu.SemaphoreType.DMA((sp_count,))),
        flops=2 * packed8 * WIDE * TOK * 2,
        moved=2 * (packed8 * WIDE + TOK * model),
    )(ids, left, combine, back_packed)
    return (
        grad_in,
        grad_gate_weight[None],
        grad_up_weight[None],
        grad_down_weight[None],
        grad_probs.T,
    )


def solution(mesh):
    placed = (
        P(("ep", "sp"), None),
        P(("ep", "sp"), None),
        P(("ep", "sp"), None),
        P(("ep", "sp"), None),
        P("ep", "sp", None),
        P("ep", "sp", None),
        P("ep", None, "sp"),
    )
    return jax.shard_map(
        on_device,
        mesh=mesh,
        in_specs=placed,
        out_specs=(
            P(("ep", "sp"), None),
            P("ep", "sp", None),
            P("ep", "sp", None),
            P("ep", None, "sp"),
            P(("ep", "sp"), None),
        ),
        check_vma=False,
    )
```

```python
import functools

import jax
import jax.numpy as jnp
from jax import lax
from jax.experimental import pallas as pl
from jax.experimental.pallas import tpu as pltpu
from jax.sharding import PartitionSpec as P

CAP = 6
EXPERTS = 32
TOK = 128
TOP = 8
WIDE = 1280
TAIL = 384
QUARTER = WIDE + TAIL
PACKED = 8
BLOCK = 32
SLOTS = BLOCK * CAP
ROWS8 = BLOCK * PACKED
RING = 4
MIB = 1 << 20
BF16 = jnp.bfloat16
F32 = jnp.float32


def iota(shape, dim):
    return lax.broadcasted_iota(jnp.int32, shape, dim)


def product(a, b):
    return jnp.dot(a, b, preferred_element_type=F32)


def product_t(a, b):
    return lax.dot_general(a, b, (((1,), (1,)), ((), ())), preferred_element_type=F32)


def one_hot(mask):
    return jnp.where(mask, 1.0, 0.0)


def ranked(ids, probs=None):
    expert = iota((EXPERTS, TOK), 0)
    member = jnp.zeros((EXPERTS, TOK), F32)
    weight = jnp.zeros((EXPERTS, TOK), F32)
    for k in range(TOP):
        hit = ids[k : k + 1, :] == expert
        member = member + jnp.where(hit, 1.0, 0.0)
        if probs is not None:
            weight = weight + jnp.where(hit, probs[k : k + 1, :], 0.0)
    member = member.astype(BF16)
    before = one_hot(iota((TOK, TOK), 0) < iota((TOK, TOK), 1)).astype(BF16)
    rank = jnp.where(member > 0.5, product(member, before), -1.0).astype(BF16)
    widen = one_hot(iota((ROWS8, EXPERTS), 0) // PACKED == iota((ROWS8, EXPERTS), 1)).astype(BF16)
    rank8 = product(widen, rank)
    weight8 = None if probs is None else product(widen, weight.astype(BF16))
    return iota((ROWS8, TOK), 0) % PACKED, rank8, weight8


def tables(ids, left_ref):
    place, rank8, _ = ranked(ids)
    own = one_hot((rank8 == place.astype(F32)) & (place < CAP))
    for g in range(3):
        goal = (place - CAP) * 3 + g
        tail = one_hot((rank8 == goal.astype(F32)) & (place >= CAP))
        left_ref[g] = jnp.concatenate([own, tail], axis=1).astype(BF16)


def late_tables(ids, probs, left_ref, combine_ref, spare_ref):
    _, _, weight8 = ranked(ids, probs)
    own = left_ref[0, :, :TOK].astype(F32)
    combine_ref[0] = own.T.astype(BF16)
    for g in range(3):
        combine_ref[g + 1] = left_ref[g, :, TOK:].astype(F32).T.astype(BF16)
    prob = jnp.sum(own * weight8, axis=1, keepdims=True)
    row = iota((ROWS8, 128), 0)
    diagonal = jnp.where(row % PACKED == iota((ROWS8, 128), 1), prob, 0.0).astype(BF16)
    r = iota((ROWS8, ROWS8), 0)
    c = iota((ROWS8, ROWS8), 1)
    lift = one_hot((r // PACKED == c // PACKED) & (r % PACKED == CAP)).astype(BF16)
    spare_ref[...] = product(lift, diagonal).astype(BF16)


def spread(left_ref, x_ref, out_ref):
    rest = x_ref[:, WIDE:]
    for g in range(3):
        cols = pl.ds(g * TAIL, TAIL)
        right = jnp.concatenate([x_ref[:, cols], rest], axis=0)
        out_ref[:, cols] = product(left_ref[g], right).astype(BF16)
    return product(left_ref[0][:, :TOK], x_ref[:, 3 * TAIL : WIDE])


def spread_x_kernel(ids_ref, x_ref, out_ref, left_ref):
    @pl.when(pl.program_id(0) == 0)
    def _():
        tables(ids_ref[...], left_ref)

    out_ref[:, 3 * TAIL :] = spread(left_ref, x_ref, out_ref).astype(BF16)


def spread_dy_kernel(ids_ref, probs_ref, left_ref, x_ref, out_ref, combine_ref, spare_ref):
    @pl.when(pl.program_id(0) == 0)
    def _():
        late_tables(ids_ref[...], probs_ref[...], left_ref, combine_ref, spare_ref)

    last = spread(left_ref, x_ref, out_ref)
    out_ref[:, 3 * TAIL :] = last.astype(BF16) + spare_ref[...]


def unpack_masks(main_ref, tail_ref):
    r = iota((SLOTS, ROWS8), 0)
    c = iota((SLOTS, ROWS8), 1)
    same = r // CAP == c // PACKED
    slot = r % CAP
    place = c % PACKED
    main_ref[...] = one_hot(same & (slot == place)).astype(BF16)
    for g in range(3):
        tail = one_hot(same & (place >= CAP) & (slot == (place - CAP) * 3 + g))
        tail_ref[:, g * ROWS8 : (g + 1) * ROWS8] = tail.astype(BF16)


def stacked(packed):
    return jnp.concatenate([packed[:, g * TAIL : (g + 1) * TAIL] for g in range(3)], axis=0)


def unpack(main_ref, tail_ref, packed, rows_ref):
    rows_ref[:, :WIDE] = product(main_ref[...], packed).astype(BF16)
    rows_ref[:, WIDE:] = product(tail_ref[...], stacked(packed)).astype(BF16)


def unpack_all(packed_ref, rows_ref, main_ref, tail_ref):
    for j in range(packed_ref.shape[0] // ROWS8):
        rows = rows_ref.at[pl.ds(j * SLOTS, SLOTS)]
        unpack(main_ref, tail_ref, packed_ref[pl.ds(j * ROWS8, ROWS8), :], rows)


def shares(source, held, sems):
    count = sems.shape[0]
    rows = held.shape[0] // count
    parts = [pl.ds(i * rows, rows) for i in range(count)]
    return [
        pltpu.make_async_copy(source.at[part], held.at[part], sems.at[i])
        for i, part in enumerate(parts)
    ]


def start(copies):
    for copy in copies:
        copy.start()


def finish(copies):
    for copy in copies:
        copy.wait()


def ring_place(n):
    return jnp.bitwise_and(lax.axis_index("sp").astype(jnp.int32) + n, RING - 1)


def span(at, rows):
    return pl.ds(pl.multiple_of(at * rows, rows), rows)


def gate_up_kernel(
    packed_hbm,
    gate_hbm,
    up_hbm,
    rows_ref,
    parts_ref,
    packed_ref,
    packed_sem,
    gate_ref,
    up_ref,
    gate_sem,
    up_sem,
    *masks,
):
    step = pl.program_id(0)
    weights = ((gate_hbm, gate_ref, gate_sem), (up_hbm, up_ref, up_sem))
    rows8 = packed_ref.shape[0] // 2
    pieces = [
        pltpu.make_async_copy(
            packed_hbm.at[pl.ds(j * rows8, rows8)],
            packed_ref.at[pl.ds(j * rows8, rows8)],
            packed_sem.at[j],
        )
        for j in range(2)
    ]

    @pl.when(step == 0)
    def _():
        pieces[0].start()
        for weight in weights:
            start(shares(*weight))
        pieces[1].start()
        unpack_masks(*masks)

    for j in range(2):

        @pl.when(step == j)
        def _(j=j):
            pieces[j].wait()

    unpack_all(packed_ref.at[span(step, rows8)], rows_ref, *masks)
    hidden = gate_ref.shape[1]
    for j, weight in enumerate(weights):

        @pl.when(step == 0)
        def _(weight=weight):
            finish(shares(*weight))

        cols = pl.ds(j * hidden, hidden)
        parts_ref[:, cols] = product(rows_ref[...], weight[1][...]).astype(BF16)


def back_parts(rows_ref, down_ref, copies, outs):
    width = down_ref.shape[0] // len(copies)
    for j, copy in enumerate(copies):
        copy.wait()
        cols = pl.ds(j * width, width)
        part = product_t(rows_ref[...], down_ref[cols, :]).astype(BF16)
        for row, out_ref in outs:
            out_ref[:, cols] = part[row : row + out_ref.shape[0]]


def back_block_kernel(turns, packed_hbm, down_hbm, *refs):
    outs, rest = refs[:2], refs[2:]
    packed_ref, packed_sem, rows_ref, down_ref, sem, *masks = rest
    pieces = [
        pltpu.make_async_copy(
            packed_hbm.at[span(ring_place(n), ROWS8)],
            packed_ref.at[pl.ds(j * ROWS8, ROWS8)],
            packed_sem.at[j],
        )
        for j, n in enumerate(turns)
    ]
    copies = shares(down_hbm, down_ref, sem)
    start(pieces)
    start(copies)
    unpack_masks(*masks)
    finish(pieces)
    unpack_all(packed_ref, rows_ref, *masks)
    back_parts(rows_ref, down_ref, copies, ((0, outs[0]), (outs[0].shape[0], outs[1])))


def back_own_kernel(packed_ref, down_hbm, rows_ref, own_ref, prob_ref, down_ref, sem, *masks):
    copies = shares(down_hbm, down_ref, sem)
    start(copies)
    unpack_masks(*masks)
    unpack_all(packed_ref, rows_ref, *masks)
    own = ring_place(0)
    back_parts(rows_ref.at[span(own, SLOTS)], down_ref, copies, ((0, own_ref),))
    r = iota((SLOTS, ROWS8), 0)
    c = iota((SLOTS, ROWS8), 1)
    pick = one_hot((r // CAP == c // PACKED) & (c % PACKED == CAP)).astype(BF16)
    mine = iota((SLOTS, 128), 0) % CAP == iota((SLOTS, 128), 1)
    probs = product(pick, packed_ref[span(own, ROWS8), 3 * TAIL :])
    prob = jnp.sum(jnp.where(mine, probs, 0.0), axis=1, keepdims=True)
    prob_ref[...] = jnp.broadcast_to(prob, (SLOTS, 128)).astype(BF16)


def join_kernel(below_ref, above_ref, first_ref, second_ref, below_out, above_out):
    half = first_ref.shape[0]
    below_out[:half] = below_ref[:half]
    below_out[half:] = (below_ref[half:].astype(F32) + second_ref[...].astype(F32)).astype(BF16)
    above_out[:half] = (above_ref[:half].astype(F32) + first_ref[...].astype(F32)).astype(BF16)
    above_out[half:] = above_ref[half:]


def activate_kernel(
    gate_up_ref, own_ref, left_ref, right_ref, prob_ref, first_ref, second_ref, weighted_ref, slot_ref
):
    rows, hidden = own_ref.shape
    half = first_ref.shape[0]
    step = 32
    for start in range(0, rows, step):
        at = pl.ds(start, step)
        grads_ref = first_ref if start < half else second_ref
        to = pl.ds(start % half, step)
        gate = gate_up_ref[at, :hidden].astype(F32)
        up = gate_up_ref[at, hidden:].astype(F32)
        back = own_ref[at, :].astype(F32) + left_ref[at, :].astype(F32)
        back = back + right_ref[at, :].astype(F32)
        weight = prob_ref[at, :1].astype(F32)
        sigmoid = 1.0 / (1.0 + jnp.exp(-gate))
        swish = gate * sigmoid
        act = swish * up
        grad_act = weight * back
        grad_gate = grad_act * up * sigmoid * (1.0 + gate * (1.0 - sigmoid))
        grads_ref[to, :hidden] = grad_gate.astype(BF16)
        grads_ref[to, hidden:] = (grad_act * swish).astype(BF16)
        weighted_ref[at, :] = (weight * act).astype(BF16)
        slot = jnp.sum(back * act, axis=1, keepdims=True)
        mine = (start + iota((step, 128), 0)) % CAP == iota((step, 128), 1)
        slot_ref[at, :] = jnp.where(mine, slot, 0.0).astype(BF16)


def pack_group(g, rows_ref, out_ref, spare=None):
    r = iota((ROWS8, SLOTS), 0)
    c = iota((ROWS8, SLOTS), 1)
    same = r // PACKED == c // CAP
    place = r % PACKED
    slot = c % CAP
    main = one_hot(same & (slot == place)).astype(BF16)
    if g < 3:
        cols = pl.ds(g * TAIL, TAIL)
        tail = one_hot(same & (place >= CAP) & (slot == (place - CAP) * 3 + g)).astype(BF16)
        left = jnp.concatenate([main, tail], axis=1)
        right = jnp.concatenate([rows_ref[:, cols], rows_ref[:, WIDE:]], axis=0)
        out_ref[:, cols] = product(left, right).astype(BF16)
        return
    last = product(main, rows_ref[:, 3 * TAIL : WIDE])
    if spare is not None:
        lift = one_hot(same & (place == CAP)).astype(BF16)
        last = last + product(lift, spare)
    out_ref[:, 3 * TAIL :] = last.astype(BF16)


COLUMN_RUNS = ((WIDE, QUARTER, ()), (0, 2 * TAIL, (0, 1)), (2 * TAIL, WIDE, (2, 3)))


def row_grad_kernel(turns, own, held, *refs):
    halves = 2 * len(turns)
    halves_hbm, rest = refs[:halves], refs[halves:]
    gate_hbm, up_hbm, extra_ref, out_hbm, grads_ref, rows_ref, packed_ref, gate_ref, up_ref = rest[:9]
    grads_sem, gate_sem, up_sem, out_sem = rest[9:]
    hidden = gate_ref.shape[1]
    half = SLOTS // 2
    grads = [
        pltpu.make_async_copy(h, grads_ref.at[pl.ds(i * half, half)], grads_sem.at[i])
        for i, h in enumerate(halves_hbm)
    ]
    start(grads)
    pairs = []
    for i, (low, high, _) in enumerate(COLUMN_RUNS):
        run = pl.ds(low, high - low)
        pair = [pltpu.make_async_copy(gate_hbm.at[run], gate_ref.at[run], gate_sem.at[i])]
        if not held:
            pair.append(pltpu.make_async_copy(up_hbm.at[run], up_ref.at[run], up_sem.at[i]))
        start(pair)
        pairs.append(pair)
    finish(grads)
    up_ref = up_hbm if held else up_ref
    spare = extra_ref[...] if own else None
    sent = []
    for (low, high, groups), pair in zip(COLUMN_RUNS, pairs):
        finish(pair)
        run = pl.ds(low, high - low)
        rows = product_t(grads_ref[:, :hidden], gate_ref[run, :])
        rows = rows + product_t(grads_ref[:, hidden:], up_ref[run, :])
        rows_ref[:, run] = rows.astype(BF16)
        for j, n in enumerate(turns):
            there = packed_ref.at[pl.ds(j * ROWS8, ROWS8)]
            for g in groups:
                pack_group(g, rows_ref.at[pl.ds(j * SLOTS, SLOTS)], there, spare)
            if groups:
                copy = pltpu.make_async_copy(
                    there.at[:, run],
                    out_hbm.at[span(ring_place(n), ROWS8), run],
                    out_sem.at[len(sent)],
                )
                copy.start()
                sent.append(copy)
    finish(sent)


def assemble_kernel(*refs):
    halves_hbm, out_ref, sem = refs[:8], refs[8], refs[9]
    half = SLOTS // 2
    copies = []
    for i, h in enumerate(halves_hbm):
        row = pl.multiple_of(ring_place((0, RING - 1, 1, 2)[i // 2]) * SLOTS + i % 2 * half, half)
        copies.append(pltpu.make_async_copy(h, out_ref.at[pl.ds(row, half)], sem.at[i]))
    start(copies)
    finish(copies)


def combine_kernel(ids_ref, left_ref, combine_ref, packed_ref, out_hbm, probs_ref, out_ref, sem):
    tails = jnp.concatenate([combine_ref[g + 1] for g in range(3)], axis=1)
    spare = jnp.zeros((ROWS8, 128), F32)
    sent = []
    for q in range(packed_ref.shape[0] // ROWS8):
        rows = pl.ds(q * ROWS8, ROWS8)
        cols = pl.ds(q * QUARTER, QUARTER)
        low = q * QUARTER
        out_ref[:, low : low + WIDE] = product(combine_ref[0], packed_ref[rows, :]).astype(BF16)
        rest = product(tails, stacked(packed_ref[rows, :])).astype(BF16)
        out_ref[:, low + WIDE : low + QUARTER] = rest
        copy = pltpu.make_async_copy(out_ref.at[:, cols], out_hbm.at[:, cols], sem.at[q])
        copy.start()
        sent.append(copy)
        spare = spare + packed_ref[rows, 3 * TAIL :].astype(F32)
    row = iota((ROWS8, 128), 0)
    slots = jnp.where(row % PACKED == CAP, spare, 0.0).astype(BF16)
    r = iota((ROWS8, ROWS8), 0)
    c = iota((ROWS8, ROWS8), 1)
    group = one_hot(r // PACKED == c // PACKED).astype(BF16)
    wide = product(group, slots)
    mine = iota((ROWS8, 128), 1) == row % PACKED
    column = jnp.sum(jnp.where(mine, wide, 0.0), axis=1, keepdims=True)
    value = (left_ref[0, :, :TOK].astype(F32) * column).astype(BF16)
    gather = one_hot(iota((EXPERTS, ROWS8), 1) // PACKED == iota((EXPERTS, ROWS8), 0))
    table = product(gather.astype(BF16), value)
    expert = iota((EXPERTS, TOK), 0)
    found = [
        jnp.sum(jnp.where(ids_ref[k : k + 1, :] == expert, table, 0.0), axis=0, keepdims=True)
        for k in range(TOP)
    ]
    probs_ref[...] = jnp.concatenate(found, axis=0).astype(BF16)
    finish(sent)


def call(kernel, grid, ins, outs, scratch=(), flops=0, moved=0, aliases=None):
    return pl.pallas_call(
        kernel,
        grid_spec=pltpu.PrefetchScalarGridSpec(
            num_scalar_prefetch=0,
            grid=(grid,),
            in_specs=ins,
            out_specs=[s for s, _, _ in outs],
            scratch_shapes=list(scratch),
        ),
        out_shape=[place(shape, kind) for _, (shape, kind), place in outs],
        compiler_params=pltpu.CompilerParams(
            dimension_semantics=("arbitrary",), vmem_limit_bytes=24 * MIB
        ),
        input_output_aliases=aliases or {},
        cost_estimate=pl.CostEstimate(flops=flops, bytes_accessed=moved, transcendentals=0),
    )


def whole(*shape):
    return pl.BlockSpec(shape, lambda *i: (0,) * len(shape))


def rows_of(rows, cols):
    return pl.BlockSpec((rows, cols), lambda i, *_: (i, 0))


def cols_of(rows, cols):
    return pl.BlockSpec((rows, cols), lambda i, *_: (0, i))


ANY = pl.BlockSpec(memory_space=pl.ANY)
NEAR = pl.BlockSpec(memory_space=pltpu.VMEM)


def on_device(hidden_in, grad_out, route_ids, route_probs, w_gate, w_up, w_down):
    sp_count = lax.axis_size("sp")
    pieces = lax.axis_size("ep") * sp_count
    hidden = w_gate.shape[2]
    model = hidden_in.shape[1]
    all_rows = pieces * CAP
    packed8 = pieces * PACKED
    gate_weight, up_weight, down_weight = w_gate[0], w_up[0], w_down[0]
    ids, probs = route_ids.T, route_probs.T

    def in_hbm(array):
        return pltpu.with_memory_space_constraint(array, pltpu.HBM)

    hidden_in, grad_out = in_hbm(hidden_in), in_hbm(grad_out)
    far, near = pltpu.HBM, jax.ShapeDtypeStruct
    tie = lax.optimization_barrier
    packet = (rows_of(ROWS8, WIDE), ((packed8, WIDE), BF16), far)
    x_send, left = call(
        spread_x_kernel,
        sp_count,
        [whole(TOP, TOK), cols_of(TOK, QUARTER)],
        [packet, (whole(3, ROWS8, ROWS8), ((3, ROWS8, ROWS8), BF16), far)],
        flops=2 * packed8 * WIDE * 256,
        moved=2 * (packed8 * WIDE + TOK * model),
    )(in_hbm(ids), hidden_in)
    dy_send, combine = call(
        spread_dy_kernel,
        sp_count,
        [whole(TOP, TOK), whole(TOP, TOK), whole(3, ROWS8, ROWS8), cols_of(TOK, QUARTER)],
        [packet, (whole(4, TOK, ROWS8), ((4, TOK, ROWS8), BF16), far)],
        (pltpu.VMEM((ROWS8, 128), BF16),),
        flops=2 * packed8 * WIDE * 256,
        moved=2 * (packed8 * WIDE + TOK * model),
    )(in_hbm(ids), in_hbm(probs), in_hbm(left), grad_out)

    def exchange(packed):
        pieced = packed.reshape(pieces, PACKED, WIDE)
        moved = lax.all_to_all(pieced, ("sp", "ep"), split_axis=0, concat_axis=0, tiled=True)
        return moved.reshape(packed8, WIDE)

    gate_weight, up_weight, down_weight = map(in_hbm, (gate_weight, up_weight, down_weight))
    x_packed = exchange(x_send)
    x_packed, dy_send = tie((in_hbm(x_packed), dy_send))
    dy_packed = exchange(dy_send)
    masks = (pltpu.VMEM((SLOTS, ROWS8), BF16), pltpu.VMEM((SLOTS, 3 * ROWS8), BF16))
    two_weights = (pltpu.VMEM((QUARTER, hidden), BF16),) * 2 + (pltpu.SemaphoreType.DMA((4,)),) * 2
    down_space = (pltpu.VMEM((hidden, QUARTER), BF16), pltpu.SemaphoreType.DMA((4,)))
    some_rows = all_rows // 2
    x_rows, gate_up_part = call(
        gate_up_kernel,
        2,
        [ANY, ANY, ANY],
        [
            (rows_of(some_rows, QUARTER), ((all_rows, QUARTER), BF16), far),
            (rows_of(some_rows, 2 * hidden), ((all_rows, 2 * hidden), BF16), far),
        ],
        (pltpu.VMEM((packed8, WIDE), BF16), pltpu.SemaphoreType.DMA((2,)), *two_weights, *masks),
        flops=4 * all_rows * QUARTER * hidden,
        moved=2 * (packed8 * WIDE + 2 * QUARTER * hidden + all_rows * (QUARTER + 2 * hidden)),
    )(x_packed, gate_weight, up_weight)
    gate_up = lax.psum_scatter(gate_up_part, "sp", scatter_dimension=0, tiled=True)
    own_rows = all_rows // sp_count
    half = own_rows // 2
    upward = [(i, (i + 1) % sp_count) for i in range(sp_count)]
    downward = [(i, (i - 1) % sp_count) for i in range(sp_count)]

    def both_ways(up, down):
        return lax.ppermute(up, "sp", upward), lax.ppermute(down, "sp", downward)

    dy_packed, _ = tie((dy_packed, gate_up_part))
    piece = ((half, hidden), BF16)
    block = ((own_rows, hidden), BF16)

    def back_space(turns):
        return (
            pltpu.VMEM((turns * ROWS8, WIDE), BF16),
            pltpu.SemaphoreType.DMA((turns,)),
            pltpu.VMEM((turns * SLOTS, QUARTER), BF16),
            *down_space,
            *masks,
        )

    far_first, far_second = call(
        functools.partial(back_block_kernel, (2,)),
        1,
        [ANY, ANY],
        [(whole(*piece[0]), piece, near)] * 2,
        back_space(1),
        flops=32 * 2 * all_rows * QUARTER * hidden,
        moved=2 * (packed8 * WIDE + QUARTER * hidden + all_rows * QUARTER),
    )(dy_packed, down_weight)
    far_first, far_second = both_ways(far_first, far_second)
    back_below, back_above = call(
        functools.partial(back_block_kernel, (sp_count - 1, 1)),
        1,
        [ANY, ANY],
        [(whole(*block[0]), block, near)] * 2,
        back_space(2),
        flops=2 * 2 * own_rows * QUARTER * hidden,
        moved=2 * (QUARTER * hidden + 2 * ROWS8 * WIDE + 2 * own_rows * hidden),
    )(dy_packed, down_weight)
    back_below, back_above = call(
        join_kernel,
        1,
        [whole(*block[0])] * 2 + [whole(*piece[0])] * 2,
        [(whole(*block[0]), block, near)] * 2,
        moved=2 * 5 * own_rows * hidden,
    )(back_below, back_above, far_first, far_second)
    left_part, right_part = both_ways(back_above, back_below)
    dy_late, _ = tie((dy_packed, back_above))
    dy_rows, back_own, prob_own = call(
        back_own_kernel,
        1,
        [whole(packed8, WIDE), ANY],
        [
            (whole(all_rows, QUARTER), ((all_rows, QUARTER), BF16), far),
            (whole(*block[0]), block, far),
            (whole(own_rows, 128), ((own_rows, 128), BF16), far),
        ],
        (*down_space, *masks),
        flops=2 * own_rows * QUARTER * hidden,
        moved=2 * (QUARTER * hidden + packed8 * WIDE + all_rows * QUARTER + own_rows * hidden),
    )(dy_late, down_weight)
    first, second, weighted_own, slot_own = call(
        activate_kernel,
        1,
        [whole(own_rows, 2 * hidden)] + [whole(*block[0])] * 3 + [whole(own_rows, 128)],
        [
            (whole(half, 2 * hidden), ((half, 2 * hidden), BF16), far),
            (whole(half, 2 * hidden), ((half, 2 * hidden), BF16), far),
            (whole(own_rows, hidden), ((own_rows, hidden), BF16), far),
            (whole(own_rows, 128), ((own_rows, 128), BF16), far),
        ],
        flops=20 * own_rows * hidden,
        moved=12 * own_rows * hidden,
    )(in_hbm(gate_up), in_hbm(back_own), left_part, right_part, in_hbm(prob_own))
    below_first, above_second = both_ways(first, second)
    below_second, above_first = both_ways(second, first)

    def row_grad(turns, grads, extra, own_block=False, held=False):
        count = len(grads)
        blocks = len(turns)
        dma = pltpu.SemaphoreType.DMA
        return call(
            functools.partial(row_grad_kernel, turns, own_block, held),
            1,
            [ANY] * (count + 1)
            + [NEAR if held else ANY, whole(own_rows, 128) if own_block else ANY],
            [(ANY, ((packed8, WIDE), BF16), far)],
            (
                pltpu.VMEM((blocks * SLOTS, 2 * hidden), BF16),
                pltpu.VMEM((blocks * SLOTS, QUARTER), BF16),
                pltpu.VMEM((blocks * ROWS8, WIDE), BF16),
                pltpu.VMEM((QUARTER, hidden), BF16),
                pltpu.VMEM((QUARTER, hidden), BF16),
                dma((count,)),
                dma((3,)),
                dma((3,)),
                dma((2 * blocks,)),
            ),
            aliases={} if own_block else {count + 2: 0},
            flops=4 * blocks * own_rows * QUARTER * hidden,
            moved=2 * (2 * QUARTER * hidden + blocks * (ROWS8 * WIDE + own_rows * 2 * hidden)),
        )(*grads, gate_weight, w_up[0] if held else up_weight, extra)[0]

    own_halves = (in_hbm(first), in_hbm(second))
    back_send = row_grad((0,), own_halves, in_hbm(slot_own), own_block=True)
    below_first, above_second, back_send = tie((below_first, above_second, back_send))
    across_first, across_second = both_ways(below_first, above_second)
    near_halves = (below_first, below_second, above_first, above_second)
    back_send = row_grad((sp_count - 1, 1), near_halves, back_send)
    across_first, across_second, back_send = tie((across_first, across_second, back_send))
    weighted_own, _, _ = tie((weighted_own, below_second, above_first))
    weighted = lax.all_gather(weighted_own, "sp", axis=0, tiled=True)
    back_send = row_grad((2,), (across_first, across_second), back_send, held=True)
    back_packed = exchange(back_send)
    (grads_all,) = call(
        assemble_kernel,
        1,
        [ANY] * 8,
        [(whole(all_rows, 2 * hidden), ((all_rows, 2 * hidden), BF16), near)],
        (pltpu.SemaphoreType.DMA((8,)),),
        moved=2 * 2 * all_rows * 2 * hidden,
    )(*tie((*own_halves, *near_halves, across_first, across_second, back_send))[:8])
    contract_rows = (((0,), (0,)), ((), ()))

    def over_rows(a, b):
        return lax.dot_general(a, b, contract_rows, preferred_element_type=F32).astype(BF16)

    grad_gate_weight = over_rows(x_rows, grads_all[:, :hidden])
    grad_up_weight = over_rows(x_rows, grads_all[:, hidden:])
    grad_down_weight = over_rows(weighted, dy_rows)
    grad_in, grad_probs = call(
        combine_kernel,
        1,
        [NEAR, NEAR, NEAR, NEAR],
        [
            (ANY, ((TOK, model), BF16), far),
            (whole(TOP, TOK), ((TOP, TOK), BF16), near),
        ],
        (pltpu.VMEM((TOK, model), BF16), pltpu.SemaphoreType.DMA((sp_count,))),
        flops=2 * packed8 * WIDE * TOK * 2,
        moved=2 * (packed8 * WIDE + TOK * model),
    )(ids, left, combine, back_packed)
    return (
        grad_in,
        grad_gate_weight[None],
        grad_up_weight[None],
        grad_down_weight[None],
        grad_probs.T,
    )


def solution(mesh):
    placed = (
        P(("ep", "sp"), None),
        P(("ep", "sp"), None),
        P(("ep", "sp"), None),
        P(("ep", "sp"), None),
        P("ep", "sp", None),
        P("ep", "sp", None),
        P("ep", None, "sp"),
    )
    return jax.shard_map(
        on_device,
        mesh=mesh,
        in_specs=placed,
        out_specs=(
            P(("ep", "sp"), None),
            P("ep", "sp", None),
            P("ep", "sp", None),
            P("ep", None, "sp"),
            P(("ep", "sp"), None),
        ),
        check_vma=False,
    )
```
